256 devices in a mesh: comp: 16 (over x, y_lo, core), dom: 16 (over y_hi, z).
Axes of the slice: x: 4, y: 4 (y_hi: 2, y_lo: 2; y = y_hi * 2 + y_lo), z: 8, core: 2. Of those that a mesh axis runs over, the one named last changes fastest.
Arguments:
- density: float32 [16, 32, 16, 16, 256], P('comp', 'dom'), may hold values from -6 to 6
- velocity: bfloat16 [16, 6, 32, 16, 16, 256], P('comp', None, 'dom'), may hold values from -0.099609375 to 0.099609375
- coefficients: int32 [16], replicated, may hold values from -1 to 1, as said below
- owner_lists: int32 [388, 16], replicated, may hold values from -1 to 511, as said below
Outputs:
- combined: float32 [16, 32, 16, 16, 256], P('comp', 'dom')
The draws below stay inside these ranges and needn't reach their ends.
Inputs may be any that keep to these rules, and one draw needn't show every extreme that they name: `coefficients`: each is -1 or 1. `owner_lists`: every slab number c * 32 + s appears in exactly one row; within a row the entries are distinct and ascending, padding -1 follows them, and every row has at least one entry; no row names two slabs of one component; 4 rows name all 16 components; exactly 68 rows have more than one entry, and those that do not name all components have exactly two; every component has exactly 12 slabs in rows with more than one entry.
All inputs are finite; a program needn't handle non-finite values.
Results may differ from the reference program's by a relative error of at most 0.0003.
Values may be sent and summed in bfloat16 or wider, within the bound.
A program may use at most 64 MiB of HBM per device.

```python
import jax
import jax.numpy as jnp
import numpy as np
from jax import lax

GRID_A = 32
GRID_B = 16
GRID_C = 16
GRID_D = 8
GRID_E = 8
GRID_F = 4
STEPS = 4
SHARED = 4
BORROWED = 4
COMPS = 16
OWN_SLABS = 24
SUBSPACE_BLOCKS = 388


def slab_labels(key):
    comp_order = jax.random.permutation(jax.random.fold_in(key, 2), COMPS).astype(jnp.int32)
    comp_place = jnp.zeros((COMPS,), jnp.int32).at[comp_order].set(jnp.arange(COMPS, dtype=jnp.int32))
    offsets = (jax.random.permutation(jax.random.fold_in(key, 3), COMPS - 1)[:BORROWED] + 1).astype(jnp.int32)

    def for_component(component):
        comp_key = jax.random.fold_in(key, component)
        ordering = jax.random.permutation(jax.random.fold_in(comp_key, 1), GRID_A)
        roles = jnp.arange(GRID_A, dtype=jnp.int32)
        borrowed_index = jnp.clip(roles - SHARED - OWN_SLABS, 0, BORROWED - 1)

        def destination_for(lent_index):
            return comp_order[(comp_place[component] + offsets[lent_index]) % COMPS]

        def pick_for(lent_index):
            lent_target = destination_for(lent_index)
            chosen = jax.random.permutation(jax.random.fold_in(key, 1000 + lent_target), OWN_SLABS)
            return chosen[lent_index].astype(jnp.int32)
        lent_indices = jnp.arange(BORROWED, dtype=jnp.int32)
        targets = jax.vmap(destination_for)(lent_indices)
        picks = jax.vmap(pick_for)(lent_indices)
        own_label = SHARED + component * OWN_SLABS + roles - SHARED
        lent_label = SHARED + targets[borrowed_index] * OWN_SLABS + picks[borrowed_index]
        label = jnp.where(roles < SHARED, roles, jnp.where(roles < SHARED + OWN_SLABS, own_label, lent_label))
        return jnp.zeros((GRID_A,), jnp.int32).at[ordering].set(label.astype(jnp.int32))
    block_labels = jax.vmap(for_component)(jnp.arange(COMPS, dtype=jnp.int32)).reshape(-1)
    relabel_blocks = jax.random.permutation(jax.random.fold_in(key, 4), SUBSPACE_BLOCKS).astype(jnp.int32)
    return relabel_blocks[block_labels]


def draw_owner_lists(key, part):
    block_labels = slab_labels(jax.random.fold_in(key, 11))
    blocks = jnp.arange(SUBSPACE_BLOCKS, dtype=jnp.int32)
    hits = block_labels[None, :] == blocks[:, None]
    ranking = jnp.argsort(jnp.where(hits, 0, 1).astype(jnp.int32), axis=1, stable=True)[:, :COMPS]
    counts = jnp.sum(hits.astype(jnp.int32), axis=1)
    slots = jnp.arange(COMPS, dtype=jnp.int32)
    return jnp.where(slots[None, :] < counts[:, None], ranking, -1).astype(jnp.int32)


def draw_coefficients(key, part):
    return (2 * jax.random.randint(jax.random.fold_in(key, 7), (COMPS,), 0, 2) - 1).astype(jnp.int32)


def shard_levels(stream_key, shape, cuts, low, top_value):
    def one(axis_at, shards_of):
        draws = jax.random.uniform(jax.random.fold_in(jax.random.fold_in(stream_key, 6), axis_at), (shards_of,), jnp.float32, low / len(cuts), top_value / len(cuts))
        return jnp.repeat(jnp.exp(draws), shape[axis_at] // shards_of).reshape((-1,) + (1,) * (len(shape) - axis_at - 1))

    factor_of = one(*cuts[0])
    for cut in cuts[1:]:
        factor_of = factor_of * one(*cut)
    return factor_of


def gaussian(rng, shape, width, reach, cuts=(), kind=jnp.bfloat16):
    level = shard_levels(rng, shape, cuts, -0.22, 0.18) if cuts else 1.0
    values = jax.random.normal(rng, shape, jnp.float32) * width * level
    return jnp.minimum(jnp.maximum(values, -reach), reach).astype(kind)


def setup_inputs(seed: int = 0) -> dict:
    streams_of = jax.random.split(jax.random.key(seed), 5)
    return {
        "density": gaussian(streams_of[0], (COMPS, GRID_A, GRID_B, GRID_C, GRID_D * GRID_E * GRID_F), 1.0, 6.0, ((0, 16), (1, 16)), jnp.float32),
        "velocity": jnp.clip(jax.random.uniform(streams_of[1], (COMPS, 6, GRID_A, GRID_B, GRID_C, GRID_D * GRID_E * GRID_F), jnp.float32, -0.099609375, 0.099609375) * shard_levels(streams_of[1], (COMPS, 6, GRID_A, GRID_B, GRID_C, GRID_D * GRID_E * GRID_F), ((0, 16), (2, 16)), -0.4, 0.0), -0.099609375, 0.099609375).astype(jnp.bfloat16),
        "coefficients": draw_coefficients(jax.random.fold_in(streams_of[4], 71), 0),
        "owner_lists": draw_owner_lists(jax.random.fold_in(streams_of[4], 71), 0),
    }


def surplus_matrix(points):
    matrix = np.eye(points)
    for position in range(1, points):
        spacing = position & (-position)
        matrix[position, (position - spacing) % points] -= 0.5
        matrix[position, (position + spacing) % points] -= 0.5
    return matrix


def nodal_matrix(points):
    matrix = np.zeros((points, points))
    matrix[0, 0] = 1.0
    spacing = points // 2
    while spacing >= 1:
        for position in range(spacing, points, 2 * spacing):
            matrix[position] = 0.5 * (matrix[(position - spacing) % points] + matrix[(position + spacing) % points])
            matrix[position, position] += 1.0
        spacing = spacing // 2
    return matrix


def along_axis(values, matrix, dimension):
    moved = jnp.tensordot(values, jnp.asarray(matrix, values.dtype), axes=([dimension], [1]), precision=lax.Precision.HIGHEST)
    return jnp.moveaxis(moved, -1, dimension)


def advance(values, speeds):
    full_shape = (COMPS, GRID_A, GRID_B, GRID_C, GRID_D, GRID_E, GRID_F)
    current = values.reshape(full_shape)
    rates = speeds.astype(values.dtype).reshape((COMPS, 6) + full_shape[1:])
    updated = current
    for dimension in range(6):
        forward_sweep = jnp.roll(current, -1, dimension + 1)
        backward = jnp.roll(current, 1, dimension + 1)
        updated = updated + 0.06 * (forward_sweep - 2.0 * current + backward) - 0.5 * rates[:, dimension] * (forward_sweep - backward)
    return updated.reshape(values.shape)


def slab_blocks(owner_lists):
    block_labels = jnp.broadcast_to(jnp.arange(SUBSPACE_BLOCKS, dtype=jnp.int32)[:, None], owner_lists.shape)
    targets = jnp.where(owner_lists >= 0, owner_lists, COMPS * GRID_A).astype(jnp.int32)
    empty = jnp.zeros((COMPS * GRID_A,), jnp.int32)
    return empty.at[targets.reshape(-1)].set(block_labels.reshape(-1), mode="drop")


def reference(density, velocity, coefficients, owner_lists):
    advected = density
    for time_step in range(STEPS):
        advected = advance(advected, velocity)
    inner_surplus = np.kron(np.kron(surplus_matrix(GRID_D), surplus_matrix(GRID_E)), surplus_matrix(GRID_F))
    surplus = along_axis(advected, inner_surplus, 4)
    surplus = along_axis(surplus, surplus_matrix(GRID_B), 2)
    surplus = along_axis(surplus, surplus_matrix(GRID_C), 3)
    surplus = along_axis(surplus, surplus_matrix(GRID_A), 1)
    slab_rows = surplus.reshape(COMPS * GRID_A, -1)
    weights = jnp.repeat(coefficients.astype(density.dtype), GRID_A)
    block_of = slab_blocks(owner_lists)
    block_sum = jax.ops.segment_sum(slab_rows * weights[:, None], block_of, num_segments=SUBSPACE_BLOCKS)
    merged = block_sum[block_of].reshape(surplus.shape)
    inner_nodal = np.kron(np.kron(nodal_matrix(GRID_D), nodal_matrix(GRID_E)), nodal_matrix(GRID_F))
    result = along_axis(merged, nodal_matrix(GRID_A), 1)
    result = along_axis(result, inner_nodal, 4)
    result = along_axis(result, nodal_matrix(GRID_B), 2)
    result = along_axis(result, nodal_matrix(GRID_C), 3)
    return result
```

```python
import functools

import jax
import jax.numpy as jnp
import numpy as np
from jax import lax
from jax.experimental import pallas as pl
from jax.experimental.pallas import tpu as pltpu
from jax.sharding import PartitionSpec as P

STEPS = 4
E_STRIDE, E_EXT = 4, 8
F_STRIDE, F_EXT = 1, 4
ROWS = 16
USED = 12
CHUNKS = 4


def tables(owner_lists, coefficients, n_comp, n_slab, me):
    blocks = owner_lists.shape[0]
    shared = owner_lists[:, 1:2] >= 0
    keys = jnp.where(shared, owner_lists, -1)
    ids = jnp.arange(1, blocks + 1, dtype=jnp.int32)
    slabs = jnp.arange(n_comp * n_slab, dtype=jnp.int32)
    hit = jnp.where(keys[None] == slabs[:, None, None], ids[None, :, None], 0)
    block = jnp.sum(hit, axis=(1, 2)).reshape(n_comp, n_slab)
    multi = block > 0
    place = jnp.arange(n_slab, dtype=jnp.int32)
    before = place[None, :] < place[:, None]
    rank = jnp.sum(jnp.where(before[None] & multi[:, None, :], 1, 0), axis=2)
    slot = jnp.arange(ROWS, dtype=jnp.int32)
    chosen = multi[:, None, :] & (rank[:, None, :] == slot[None, :, None])
    row_block = jnp.sum(jnp.where(chosen, block[:, None, :], 0), axis=2)
    row_place = jnp.sum(jnp.where(chosen, place[None, None, :], 0), axis=2)
    my_rows = lax.dynamic_slice_in_dim(row_place, me, 1)[0]
    my_slot = jnp.where(
        lax.dynamic_slice_in_dim(multi, me, 1)[0],
        lax.dynamic_slice_in_dim(rank, me, 1)[0],
        USED,
    )
    weight = jnp.broadcast_to(coefficients[:, None], (n_comp, ROWS))
    flat = row_block.reshape(1, -1)
    return (
        my_rows,
        my_slot,
        flat.reshape(-1, 1),
        flat,
        weight.reshape(1, -1),
        lax.dynamic_slice_in_dim(coefficients, me, 1),
    )


def stencil(cur, low, high, left, right, rates, masks):
    e_last, e_first, f_last, f_first, d_low, d_high = masks
    out = []
    down = [pltpu.roll(x, 32, 1) for x in cur]
    up = [pltpu.roll(x, 96, 1) for x in cur]
    for h in range(2):
        x = cur[h]
        pairs = [(high[h], low[h]), (right[h], left[h])]
        n = x.shape[0]
        pairs.append((pltpu.roll(x, n - 1, 0), pltpu.roll(x, 1, 0)))
        pairs.append(
            (jnp.where(d_high, up[1 - h], up[h]), jnp.where(d_low, down[1 - h], down[h]))
        )
        pairs.append(
            (
                jnp.where(e_last, pltpu.roll(x, 28, 1), pltpu.roll(x, 124, 1)),
                jnp.where(e_first, pltpu.roll(x, 100, 1), pltpu.roll(x, 4, 1)),
            )
        )
        pairs.append(
            (
                jnp.where(f_last, pltpu.roll(x, 3, 1), pltpu.roll(x, 127, 1)),
                jnp.where(f_first, pltpu.roll(x, 125, 1), pltpu.roll(x, 1, 1)),
            )
        )
        total = None
        drift = None
        for d, (fwd, bwd) in enumerate(pairs):
            s = fwd + bwd
            m = rates[h][d] * (fwd - bwd)
            total = s if total is None else total + s
            drift = m if drift is None else drift + m
        out.append(0.28 * x + 0.06 * total - 0.5 * drift)
    return out


def kernel(
    nc, nd,
    rows_ref, slot_ref, own_ref, bcol_ref, brow_ref, wrow_ref, dens_ref, vel_ref,
    out_ref,
    ubuf, hfirst, hs, hr, line, tsend, tall, eback, erecv, ez, osend, orecv, mix,
    hs_sem, hr_sem, a_sem, b_sem,
):
    mc = lax.axis_index("comp")
    md = lax.axis_index("dom")
    nb = dens_ref.shape[1]
    size = nb // CHUNKS
    up_d = lax.rem(md + 1, nd)
    dn_d = lax.rem(md + nd - 1, nd)

    barrier = pltpu.get_barrier_semaphore()

    @pl.loop(1, nd)
    def _(i):
        pl.semaphore_signal(barrier, inc=1, device_id={"dom": lax.rem(md + i, nd)})

    @pl.loop(1, nc)
    def _(i):
        pl.semaphore_signal(barrier, inc=1, device_id={"comp": lax.rem(mc + i, nc)})

    def halo(step, way, ch):
        part = pl.ds(ch * size, size)
        if step == 0:
            src, dst = dens_ref.at[1 - way, part], hfirst.at[way, part]
        else:
            src, dst = hs.at[step - 1, way, part], hr.at[step - 1, way, part]
        return pltpu.make_async_remote_copy(
            src_ref=src,
            dst_ref=dst,
            send_sem=hs_sem.at[step, way, ch],
            recv_sem=hr_sem.at[step, way, ch],
            device_id={"dom": up_d if way == 0 else dn_d},
        )

    pl.semaphore_wait(barrier, nd + nc - 2)

    @pl.loop(0, CHUNKS)
    def _(ch):
        halo(0, 0, ch).start()
        halo(0, 1, ch).start()

    same = (bcol_ref[...] == brow_ref[...]) & (brow_ref[...] > 0)
    width = nc * ROWS
    far = (lax.broadcasted_iota(jnp.int32, (width, width), 0) // ROWS) != (
        lax.broadcasted_iota(jnp.int32, (width, width), 1) // ROWS
    )
    mix[...] = jnp.where(
        same & far, wrow_ref[...].astype(jnp.float32), 0.0
    ).astype(jnp.bfloat16)

    nrow = dens_ref.shape[2]
    lane = lax.broadcasted_iota(jnp.int32, (nrow, 128), 1)
    e_idx = (lane // E_STRIDE) % E_EXT
    f_idx = lane % F_EXT
    masks = (
        e_idx == E_EXT - 1, e_idx == 0, f_idx == F_EXT - 1, f_idx == 0,
        lane < 32, lane >= 96,
    )

    def halves(ref, *idx):
        return [ref[(*idx, slice(None), pl.ds(h * 128, 128))].astype(jnp.float32) for h in range(2)]

    for step in range(STEPS):
        src = dens_ref if step == 0 else ubuf.at[(step - 1) % 2]
        dst = ubuf.at[step % 2]

        @pl.loop(0, CHUNKS)
        def _(ch):
            halo(step, 0, ch).wait_recv()
            halo(step, 1, ch).wait_recv()

            @pl.loop(0, size)
            def _(i):
                b = ch * size + i
                bm = lax.rem(b + nb - 1, nb)
                bp = lax.rem(b + 1, nb)
                first = halves(src, 0, b)
                second = halves(src, 1, b)
                lo = halves(hfirst, 0, b) if step == 0 else halves(hr, step - 1, 0, b)
                hi = halves(hfirst, 1, b) if step == 0 else halves(hr, step - 1, 1, b)
                for p in range(2):
                    cur = first if p == 0 else second
                    rates = [
                        [
                            vel_ref[d, p, b, :, pl.ds(h * 128, 128)].astype(jnp.float32)
                            for d in range(6)
                        ]
                        for h in range(2)
                    ]
                    new = stencil(
                        cur,
                        lo if p == 0 else first,
                        second if p == 0 else hi,
                        halves(src, p, bm),
                        halves(src, p, bp),
                        rates,
                        masks,
                    )
                    for h in range(2):
                        dst[p, b, :, pl.ds(h * 128, 128)] = new[h]
                        if step < STEPS - 1:
                            hs[step, 1 - p, b, :, pl.ds(h * 128, 128)] = new[h].astype(
                                jnp.bfloat16
                            )

            if step < STEPS - 1:
                halo(step + 1, 0, ch).start()
                halo(step + 1, 1, ch).start()

    last = ubuf.at[(STEPS - 1) % 2]

    def spread(src_of, dst, phase, axis, me, peer):
        return pltpu.make_async_remote_copy(
            src_ref=src_of(peer),
            dst_ref=dst(me),
            send_sem=a_sem.at[phase, peer],
            recv_sem=b_sem.at[phase, me],
            device_id={axis: peer},
        )

    def incoming(src_of, dst, phase, axis, peer):
        return pltpu.make_async_remote_copy(
            src_ref=src_of(peer),
            dst_ref=dst(peer),
            send_sem=a_sem.at[phase, peer],
            recv_sem=b_sem.at[phase, peer],
            device_id={axis: peer},
        )

    def exchange_start(src_of, dst, phase, axis, me, n):
        @pl.loop(1, n)
        def _(i):
            spread(src_of, dst, phase, axis, me, lax.rem(me + i, n)).start()

    def exchange_wait(src_of, dst, phase, axis, me, n):
        @pl.loop(1, n)
        def _(i):
            incoming(src_of, dst, phase, axis, lax.rem(me + n - i, n)).wait_recv()

    ph0 = (lambda d: last.at[:, d], lambda d: line.at[pl.ds(2 * d, 2)], 0, "dom")
    exchange_start(*ph0, md, nd)
    for p in range(2):
        line[2 * md + p] = last[p, md]
    exchange_wait(*ph0, md, nd)

    for half in range(2):
        rows = []
        for k in range(8):
            j = half * 8 + k
            if j >= USED:
                rows.append(jnp.zeros_like(line[0]))
                continue
            s = rows_ref[j]
            h = s & (-s)
            w = jnp.where(s == 0, 0.0, 0.5)
            n = 2 * nd
            lo = (s - h) & (n - 1)
            hi = (s + h) & (n - 1)
            rows.append(line[s] - w * (line[lo] + line[hi]))
        block = jnp.stack(rows, axis=0)
        tsend[:, pl.ds(half * 8, 8), :] = jnp.swapaxes(block, 0, 1)

    ph1 = (lambda c: tsend.at[c], lambda c: tall.at[c], 1, "comp")
    exchange_start(*ph1, mc, nc)
    tall[mc] = tsend[mc]
    exchange_wait(*ph1, mc, nc)

    t = tall[...].reshape(nc * ROWS, 256)
    m = mix[...]
    acc = None
    for part in range(3):
        piece = t.astype(jnp.bfloat16)
        t = t - piece.astype(jnp.float32)
        prod = jnp.dot(m, piece, preferred_element_type=jnp.float32)
        acc = prod if acc is None else acc + prod
    eback[...] = acc.reshape(nc, ROWS, 256)

    ph2 = (lambda c: eback.at[c], lambda c: erecv.at[c], 2, "comp")
    exchange_start(*ph2, mc, nc)
    erecv[mc] = eback[mc]
    exchange_wait(*ph2, mc, nc)

    for half in range(2):
        ez[pl.ds(half * 8, 8)] = jnp.swapaxes(erecv[:, pl.ds(half * 8, 8), :], 0, 1)

    n = 2 * nd
    for q in range(4):
        if q % 2 * 8 >= nrow:
            continue
        r = (pl.ds(q % 2 * 8, min(8, nrow)), pl.ds(q // 2 * 128, 128))
        planes = {}
        planes[0] = ez[(slot_ref[0], *r)]
        gap = n // 2
        while gap >= 1:
            for s in range(gap, n, 2 * gap):
                planes[s] = ez[(slot_ref[s], *r)] + 0.5 * (
                    planes[(s - gap) % n] + planes[(s + gap) % n]
                )
            gap //= 2
        for s in range(n):
            osend[(s, *r)] = planes[s]

    ph3 = (lambda d: osend.at[pl.ds(2 * d, 2)], lambda d: orecv.at[d], 3, "dom")
    exchange_start(*ph3, md, nd)
    for p in range(2):
        orecv[md, p] = osend[2 * md + p]
    exchange_wait(*ph3, md, nd)

    own = own_ref[0].astype(jnp.float32)

    @pl.loop(0, nb)
    def _(b):
        for p in range(2):
            out_ref[p, b] = own * last[p, b] + orecv[b, p]

    @pl.loop(0, CHUNKS)
    def _(ch):
        for step in range(STEPS):
            halo(step, 0, ch).wait_send()
            halo(step, 1, ch).wait_send()

    for ph, me, k in ((ph0, md, nd), (ph1, mc, nc), (ph2, mc, nc), (ph3, md, nd)):
        @pl.loop(1, k)
        def _(i):
            spread(*ph, me, lax.rem(me + i, k)).wait_send()


def local(density, velocity, coefficients, owner_lists):
    nc = lax.axis_size("comp")
    nd = lax.axis_size("dom")
    _, planes, nb, nrow, lanes = density.shape
    tabs = tables(owner_lists, coefficients, nc, planes * nd, lax.axis_index("comp"))
    rows, slot, bcol, brow, wrow, own = tabs
    f32 = jnp.float32
    smem = pl.BlockSpec(memory_space=pltpu.SMEM)
    vmem = pl.BlockSpec(memory_space=pltpu.VMEM)
    out = pl.pallas_call(
        functools.partial(kernel, nc, nd),
        out_shape=jax.ShapeDtypeStruct((planes, nb, nrow, lanes), f32),
        in_specs=[smem, smem, smem, vmem, vmem, vmem, vmem, vmem],
        out_specs=vmem,
        scratch_shapes=[
            pltpu.VMEM((2, planes, nb, nrow, lanes), f32),
            pltpu.VMEM((2, nb, nrow, lanes), f32),
            pltpu.VMEM((STEPS - 1, 2, nb, nrow, lanes), jnp.bfloat16),
            pltpu.VMEM((STEPS - 1, 2, nb, nrow, lanes), jnp.bfloat16),
            pltpu.VMEM((planes * nd, nrow, lanes), f32),
            pltpu.VMEM((nc, ROWS, lanes), f32),
            pltpu.VMEM((nc, ROWS, lanes), f32),
            pltpu.VMEM((nc, ROWS, lanes), f32),
            pltpu.VMEM((nc, ROWS, lanes), f32),
            pltpu.VMEM((ROWS, nrow, lanes), f32),
            pltpu.VMEM((planes * nd, nrow, lanes), f32),
            pltpu.VMEM((nd, planes, nrow, lanes), f32),
            pltpu.VMEM((nc * ROWS, nc * ROWS), jnp.bfloat16),
            pltpu.SemaphoreType.DMA((STEPS, 2, CHUNKS)),
            pltpu.SemaphoreType.DMA((STEPS, 2, CHUNKS)),
            pltpu.SemaphoreType.DMA((4, max(nc, nd))),
            pltpu.SemaphoreType.DMA((4, max(nc, nd))),
        ],
        compiler_params=pltpu.CompilerParams(collective_id=0, has_side_effects=True),
    )(rows, slot, own, bcol, brow, wrow, density[0], velocity[0])
    return out[None]


def solution(mesh):
    in_specs = (
        P("comp", "dom", None, None, None),
        P("comp", None, "dom", None, None, None),
        P(),
        P(),
    )
    out_specs = P("comp", "dom", None, None, None)
    return jax.shard_map(local, mesh=mesh, in_specs=in_specs, out_specs=out_specs, check_vma=False)
```

```python
import functools

import jax
import jax.numpy as jnp
import numpy as np
from jax import lax
from jax.experimental import pallas as pl
from jax.experimental.pallas import tpu as pltpu
from jax.sharding import PartitionSpec as P

STEPS = 4
E_STRIDE, E_EXT = 4, 8
F_STRIDE, F_EXT = 1, 4
ROWS = 16
USED = 12
CHUNKS = 4


def fold(x, axis, op):
    shift = x.shape[axis] // 2
    while shift:
        x = op(x, pltpu.roll(x, shift, axis))
        shift //= 2
    return x


def tables(lists_ref, coef_ref, padded, table, comb, mix, nc, ns):
    i32 = jnp.int32
    depth, blocks = lists_ref.shape
    lane = lax.broadcasted_iota(i32, (8, 128), 1)
    sub = lax.broadcasted_iota(i32, (8, 128), 0)
    tiles = max(1, nc * ns // 128)
    per = 128 // ns
    total = nc * ns

    padded[...] = jnp.full(padded.shape, -1, i32)
    padded[:, pl.ds(0, blocks)] = lists_ref[...]
    slab = lax.broadcasted_iota(i32, (total, 128), 0)
    wide = lax.broadcasted_iota(i32, (total, 128), 1)
    number = jnp.zeros((total, 128), i32)
    for t in range(padded.shape[1] // 128):
        rows = padded[:, pl.ds(t * 128, 128)]
        own = jnp.broadcast_to(rows[:, None, :], (nc, ns, 128)).reshape(total, 128)
        found = (rows[0:1] == slab) | (rows[1:2] == slab) | (own == slab)
        found = found & (rows[1:2] >= 0)
        number = jnp.maximum(number, jnp.where(found, wide + (t * 128 + 1), 0))
    number = fold(number, 1, jnp.maximum)
    number = jnp.where(wide == slab % 128, number, 0)

    ident = jnp.zeros((8, 128), i32)
    for r in range(tiles):
        part = number[r * 128 : min(r * 128 + 128, total)]
        part = jnp.sum(part.reshape(-1, 8, 128), axis=0)
        ident = jnp.where(sub == r, fold(part, 0, jnp.add), ident)
    place = lane % ns
    one = jnp.where(ident > 0, 1, 0)
    count = one
    shift = 1
    while shift < ns:
        count = count + jnp.where(place >= shift, pltpu.roll(count, shift, 1), 0)
        shift *= 2
    slot = jnp.where(ident > 0, count - 1, USED)
    table[pl.ds(0, 8), :] = slot
    both = jnp.where(ident > 0, ident * 64 + place, 0)
    comb[pl.ds(0, 8), :] = both

    lane2 = lax.broadcasted_iota(i32, (ROWS, 128), 1)
    slot2 = lax.broadcasted_iota(i32, (ROWS, 128), 0)
    columns = []
    for c in range(nc):
        r = c // per
        row = jnp.broadcast_to(table[pl.ds(r, 1), :], (ROWS, 128))
        val = jnp.broadcast_to(comb[pl.ds(r, 1), :], (ROWS, 128))
        mine = (row == slot2) & (lane2 // ns == c % per)
        columns.append(fold(jnp.where(mine, val, 0), 1, jnp.add))

    groups = 128 // ROWS
    width = nc * ROWS
    srow = jnp.zeros((8, 128), i32)
    across = []
    for t in range(0, nc, groups):
        line = jnp.zeros((ROWS, 128), i32)
        for c in range(t, min(t + groups, nc)):
            diag = lane2 == slot2 + (c - t) * ROWS
            line = line + jnp.where(diag, columns[c], 0)
        line = fold(line[:8] + line[8:], 0, jnp.add)
        across.append(jnp.concatenate([line, line], axis=0))
        srow = jnp.where(sub == t // groups, line % 64, srow)
    table[pl.ds(8, 8), :] = srow

    span = min(128, width)
    for t, wide in enumerate(across):
        owner = lane2 // ROWS + t * groups
        weight = jnp.zeros((ROWS, 128), i32)
        for c in range(nc):
            weight = jnp.where(owner == c, coef_ref[c], weight)
        for c in range(nc):
            same = (columns[c] // 64 == wide // 64) & (wide > 0) & (owner != c)
            piece = jnp.where(same, weight, 0).astype(jnp.float32).astype(jnp.bfloat16)
            mix[pl.ds(c * ROWS, ROWS), pl.ds(t * 128, span)] = piece[:, :span]


def stencil(cur, low, high, left, right, rates, masks):
    e_last, e_first, f_last, f_first, d_low, d_high = masks
    out = []
    down = [pltpu.roll(x, 32, 1) for x in cur]
    up = [pltpu.roll(x, 96, 1) for x in cur]
    for h in range(2):
        x = cur[h]
        pairs = [(high[h], low[h]), (right[h], left[h])]
        n = x.shape[0]
        pairs.append((pltpu.roll(x, n - 1, 0), pltpu.roll(x, 1, 0)))
        pairs.append(
            (jnp.where(d_high, up[1 - h], up[h]), jnp.where(d_low, down[1 - h], down[h]))
        )
        pairs.append(
            (
                jnp.where(e_last, pltpu.roll(x, 28, 1), pltpu.roll(x, 124, 1)),
                jnp.where(e_first, pltpu.roll(x, 100, 1), pltpu.roll(x, 4, 1)),
            )
        )
        pairs.append(
            (
                jnp.where(f_last, pltpu.roll(x, 3, 1), pltpu.roll(x, 127, 1)),
                jnp.where(f_first, pltpu.roll(x, 125, 1), pltpu.roll(x, 1, 1)),
            )
        )
        total = None
        drift = None
        for d, (fwd, bwd) in enumerate(pairs):
            s = fwd + bwd
            m = rates[h][d] * (fwd - bwd)
            total = s if total is None else total + s
            drift = m if drift is None else drift + m
        out.append(0.28 * x + 0.06 * total - 0.5 * drift)
    return out


def kernel(
    nc, nd,
    coef_ref, lists_ref, dens_ref, vel_ref,
    out_ref,
    ubuf, hfirst, hs, hr, line, tsend, tall, eback, erecv, ez, osend, orecv, mix, padded, table, comb, tab,
    tab_sem, hs_sem, hr_sem, a_sem, b_sem,
):
    mc = lax.axis_index("comp")
    md = lax.axis_index("dom")
    nb = dens_ref.shape[1]
    size = nb // CHUNKS
    up_d = lax.rem(md + 1, nd)
    dn_d = lax.rem(md + nd - 1, nd)

    barrier = pltpu.get_barrier_semaphore()

    @pl.loop(1, nd)
    def _(i):
        pl.semaphore_signal(barrier, inc=1, device_id={"dom": lax.rem(md + i, nd)})

    @pl.loop(1, nc)
    def _(i):
        pl.semaphore_signal(barrier, inc=1, device_id={"comp": lax.rem(mc + i, nc)})

    def halo(step, way, ch):
        part = pl.ds(ch * size, size)
        if step == 0:
            src, dst = dens_ref.at[1 - way, part], hfirst.at[way, part]
        else:
            src, dst = hs.at[step - 1, way, part], hr.at[step - 1, way, part]
        return pltpu.make_async_remote_copy(
            src_ref=src,
            dst_ref=dst,
            send_sem=hs_sem.at[step, way, ch],
            recv_sem=hr_sem.at[step, way, ch],
            device_id={"dom": up_d if way == 0 else dn_d},
        )

    pl.semaphore_wait(barrier, nd + nc - 2)

    @pl.loop(0, CHUNKS)
    def _(ch):
        halo(0, 0, ch).start()
        halo(0, 1, ch).start()

    ns = 2 * nd
    tables(lists_ref, coef_ref, padded, table, comb, mix, nc, ns)
    fetch = pltpu.make_async_copy(table, tab, tab_sem)
    fetch.start()

    per = 128 // ns

    def slot_of(s):
        return tab[mc // per, (mc % per) * ns + s]

    def slab_of(j):
        at = mc * ROWS + j
        return tab[8 + at // 128, at % 128]

    nrow = dens_ref.shape[2]
    lane = lax.broadcasted_iota(jnp.int32, (nrow, 128), 1)
    e_idx = (lane // E_STRIDE) % E_EXT
    f_idx = lane % F_EXT
    masks = (
        e_idx == E_EXT - 1, e_idx == 0, f_idx == F_EXT - 1, f_idx == 0,
        lane < 32, lane >= 96,
    )

    def halves(ref, *idx):
        return [ref[(*idx, slice(None), pl.ds(h * 128, 128))].astype(jnp.float32) for h in range(2)]

    for step in range(STEPS):
        src = dens_ref if step == 0 else ubuf.at[(step - 1) % 2]
        dst = ubuf.at[step % 2]

        @pl.loop(0, CHUNKS)
        def _(ch):
            halo(step, 0, ch).wait_recv()
            halo(step, 1, ch).wait_recv()

            @pl.loop(0, size)
            def _(i):
                b = ch * size + i
                bm = lax.rem(b + nb - 1, nb)
                bp = lax.rem(b + 1, nb)
                first = halves(src, 0, b)
                second = halves(src, 1, b)
                lo = halves(hfirst, 0, b) if step == 0 else halves(hr, step - 1, 0, b)
                hi = halves(hfirst, 1, b) if step == 0 else halves(hr, step - 1, 1, b)
                for p in range(2):
                    cur = first if p == 0 else second
                    rates = [
                        [
                            vel_ref[d, p, b, :, pl.ds(h * 128, 128)].astype(jnp.float32)
                            for d in range(6)
                        ]
                        for h in range(2)
                    ]
                    new = stencil(
                        cur,
                        lo if p == 0 else first,
                        second if p == 0 else hi,
                        halves(src, p, bm),
                        halves(src, p, bp),
                        rates,
                        masks,
                    )
                    for h in range(2):
                        dst[p, b, :, pl.ds(h * 128, 128)] = new[h]
                        if step < STEPS - 1:
                            hs[step, 1 - p, b, :, pl.ds(h * 128, 128)] = new[h].astype(
                                jnp.bfloat16
                            )

            if step < STEPS - 1:
                halo(step + 1, 0, ch).start()
                halo(step + 1, 1, ch).start()

    last = ubuf.at[(STEPS - 1) % 2]

    def spread(src_of, dst, phase, axis, me, peer):
        return pltpu.make_async_remote_copy(
            src_ref=src_of(peer),
            dst_ref=dst(me),
            send_sem=a_sem.at[phase, peer],
            recv_sem=b_sem.at[phase, me],
            device_id={axis: peer},
        )

    def incoming(src_of, dst, phase, axis, peer):
        return pltpu.make_async_remote_copy(
            src_ref=src_of(peer),
            dst_ref=dst(peer),
            send_sem=a_sem.at[phase, peer],
            recv_sem=b_sem.at[phase, peer],
            device_id={axis: peer},
        )

    def exchange_start(src_of, dst, phase, axis, me, n):
        @pl.loop(1, n)
        def _(i):
            spread(src_of, dst, phase, axis, me, lax.rem(me + i, n)).start()

    def exchange_wait(src_of, dst, phase, axis, me, n):
        @pl.loop(1, n)
        def _(i):
            incoming(src_of, dst, phase, axis, lax.rem(me + n - i, n)).wait_recv()

    ph0 = (lambda d: last.at[:, d], lambda d: line.at[pl.ds(2 * d, 2)], 0, "dom")
    exchange_start(*ph0, md, nd)
    for p in range(2):
        line[2 * md + p] = last[p, md]
    exchange_wait(*ph0, md, nd)
    fetch.wait()

    for half in range(2):
        rows = []
        for k in range(8):
            j = half * 8 + k
            if j >= USED:
                rows.append(jnp.zeros_like(line[0]))
                continue
            s = slab_of(j)
            h = s & (-s)
            w = jnp.where(s == 0, 0.0, 0.5)
            n = 2 * nd
            lo = (s - h) & (n - 1)
            hi = (s + h) & (n - 1)
            rows.append(line[s] - w * (line[lo] + line[hi]))
        block = jnp.stack(rows, axis=0)
        tsend[:, pl.ds(half * 8, 8), :] = jnp.swapaxes(block, 0, 1)

    ph1 = (lambda c: tsend.at[c], lambda c: tall.at[c], 1, "comp")
    exchange_start(*ph1, mc, nc)
    tall[mc] = tsend[mc]
    exchange_wait(*ph1, mc, nc)

    t = tall[...].reshape(nc * ROWS, 256)
    m = mix[...]
    acc = None
    for part in range(3):
        piece = t.astype(jnp.bfloat16)
        t = t - piece.astype(jnp.float32)
        prod = jnp.dot(m, piece, preferred_element_type=jnp.float32)
        acc = prod if acc is None else acc + prod
    eback[...] = acc.reshape(nc, ROWS, 256)

    ph2 = (lambda c: eback.at[c], lambda c: erecv.at[c], 2, "comp")
    exchange_start(*ph2, mc, nc)
    erecv[mc] = eback[mc]
    exchange_wait(*ph2, mc, nc)

    for half in range(2):
        ez[pl.ds(half * 8, 8)] = jnp.swapaxes(erecv[:, pl.ds(half * 8, 8), :], 0, 1)

    n = 2 * nd
    for q in range(4):
        if q % 2 * 8 >= nrow:
            continue
        r = (pl.ds(q % 2 * 8, min(8, nrow)), pl.ds(q // 2 * 128, 128))
        planes = {}
        planes[0] = ez[(slot_of(0), *r)]
        gap = n // 2
        while gap >= 1:
            for s in range(gap, n, 2 * gap):
                planes[s] = ez[(slot_of(s), *r)] + 0.5 * (
                    planes[(s - gap) % n] + planes[(s + gap) % n]
                )
            gap //= 2
        for s in range(n):
            osend[(s, *r)] = planes[s]

    ph3 = (lambda d: osend.at[pl.ds(2 * d, 2)], lambda d: orecv.at[d], 3, "dom")
    exchange_start(*ph3, md, nd)
    for p in range(2):
        orecv[md, p] = osend[2 * md + p]
    exchange_wait(*ph3, md, nd)

    own = coef_ref[mc].astype(jnp.float32)

    @pl.loop(0, nb)
    def _(b):
        for p in range(2):
            out_ref[p, b] = own * last[p, b] + orecv[b, p]

    @pl.loop(0, CHUNKS)
    def _(ch):
        for step in range(STEPS):
            halo(step, 0, ch).wait_send()
            halo(step, 1, ch).wait_send()

    for ph, me, k in ((ph0, md, nd), (ph1, mc, nc), (ph2, mc, nc), (ph3, md, nd)):
        @pl.loop(1, k)
        def _(i):
            spread(*ph, me, lax.rem(me + i, k)).wait_send()


def local(density, velocity, coefficients, owner_lists):
    nc = lax.axis_size("comp")
    nd = lax.axis_size("dom")
    _, planes, nb, nrow, lanes = density.shape
    f32 = jnp.float32
    smem = pl.BlockSpec(memory_space=pltpu.SMEM)
    vmem = pl.BlockSpec(memory_space=pltpu.VMEM)
    out = pl.pallas_call(
        functools.partial(kernel, nc, nd),
        out_shape=jax.ShapeDtypeStruct((planes, nb, nrow, lanes), f32),
        in_specs=[smem, vmem, vmem, vmem],
        out_specs=vmem,
        scratch_shapes=[
            pltpu.VMEM((2, planes, nb, nrow, lanes), f32),
            pltpu.VMEM((2, nb, nrow, lanes), f32),
            pltpu.VMEM((STEPS - 1, 2, nb, nrow, lanes), jnp.bfloat16),
            pltpu.VMEM((STEPS - 1, 2, nb, nrow, lanes), jnp.bfloat16),
            pltpu.VMEM((planes * nd, nrow, lanes), f32),
            pltpu.VMEM((nc, ROWS, lanes), f32),
            pltpu.VMEM((nc, ROWS, lanes), f32),
            pltpu.VMEM((nc, ROWS, lanes), f32),
            pltpu.VMEM((nc, ROWS, lanes), f32),
            pltpu.VMEM((ROWS, nrow, lanes), f32),
            pltpu.VMEM((planes * nd, nrow, lanes), f32),
            pltpu.VMEM((nd, planes, nrow, lanes), f32),
            pltpu.VMEM((nc * ROWS, nc * ROWS), jnp.bfloat16),
            pltpu.VMEM((nc, pl.cdiv(owner_lists.shape[0], 128) * 128), jnp.int32),
            pltpu.VMEM((16, 128), jnp.int32),
            pltpu.VMEM((8, 128), jnp.int32),
            pltpu.SMEM((16, 128), jnp.int32),
            pltpu.SemaphoreType.DMA,
            pltpu.SemaphoreType.DMA((STEPS, 2, CHUNKS)),
            pltpu.SemaphoreType.DMA((STEPS, 2, CHUNKS)),
            pltpu.SemaphoreType.DMA((4, max(nc, nd))),
            pltpu.SemaphoreType.DMA((4, max(nc, nd))),
        ],
        compiler_params=pltpu.CompilerParams(collective_id=0, has_side_effects=True),
    )(coefficients, owner_lists.T, density[0], velocity[0])
    return out[None]


def solution(mesh):
    in_specs = (
        P("comp", "dom", None, None, None),
        P("comp", None, "dom", None, None, None),
        P(),
        P(),
    )
    out_specs = P("comp", "dom", None, None, None)
    return jax.shard_map(local, mesh=mesh, in_specs=in_specs, out_specs=out_specs, check_vma=False)
```

```python
import functools

import jax
import jax.numpy as jnp
import numpy as np
from jax import lax
from jax.experimental import pallas as pl
from jax.experimental.pallas import tpu as pltpu
from jax.sharding import PartitionSpec as P

STEPS = 4
E_STRIDE, E_EXT = 4, 8
F_STRIDE, F_EXT = 1, 4
ROWS = 16
USED = 12
CHUNKS = 4


def fold(x, axis, op):
    shift = x.shape[axis] // 2
    while shift:
        x = op(x, pltpu.roll(x, shift, axis))
        shift //= 2
    return x


def tables(lists_ref, coef_ref, padded, table, comb, mix, nc, ns):
    i32 = jnp.int32
    depth, blocks = lists_ref.shape
    lane = lax.broadcasted_iota(i32, (8, 128), 1)
    sub = lax.broadcasted_iota(i32, (8, 128), 0)
    tiles = max(1, nc * ns // 128)
    per = 128 // ns
    total = nc * ns

    padded[...] = jnp.full(padded.shape, -1, i32)
    padded[:, pl.ds(0, blocks)] = lists_ref[...]
    slab = lax.broadcasted_iota(i32, (total, 128), 0)
    wide = lax.broadcasted_iota(i32, (total, 128), 1)
    number = jnp.zeros((total, 128), i32)
    for t in range(padded.shape[1] // 128):
        rows = padded[:, pl.ds(t * 128, 128)]
        own = jnp.broadcast_to(rows[:, None, :], (nc, ns, 128)).reshape(total, 128)
        found = (rows[0:1] == slab) | (rows[1:2] == slab) | (own == slab)
        found = found & (rows[1:2] >= 0)
        number = jnp.maximum(number, jnp.where(found, wide + (t * 128 + 1), 0))
    number = fold(number, 1, jnp.maximum)
    number = jnp.where(wide == slab % 128, number, 0)

    ident = jnp.zeros((8, 128), i32)
    for r in range(tiles):
        part = number[r * 128 : min(r * 128 + 128, total)]
        part = jnp.sum(part.reshape(-1, 8, 128), axis=0)
        ident = jnp.where(sub == r, fold(part, 0, jnp.add), ident)
    place = lane % ns
    one = jnp.where(ident > 0, 1, 0)
    count = one
    shift = 1
    while shift < ns:
        count = count + jnp.where(place >= shift, pltpu.roll(count, shift, 1), 0)
        shift *= 2
    slot = jnp.where(ident > 0, count - 1, USED)
    table[pl.ds(0, 8), :] = slot
    both = jnp.where(ident > 0, ident * 64 + place, 0)
    comb[pl.ds(0, 8), :] = both

    lane2 = lax.broadcasted_iota(i32, (ROWS, 128), 1)
    slot2 = lax.broadcasted_iota(i32, (ROWS, 128), 0)
    columns = []
    for c in range(nc):
        r = c // per
        row = jnp.broadcast_to(table[pl.ds(r, 1), :], (ROWS, 128))
        val = jnp.broadcast_to(comb[pl.ds(r, 1), :], (ROWS, 128))
        mine = (row == slot2) & (lane2 // ns == c % per)
        columns.append(fold(jnp.where(mine, val, 0), 1, jnp.add))

    groups = 128 // ROWS
    width = nc * ROWS
    srow = jnp.zeros((8, 128), i32)
    across = []
    for t in range(0, nc, groups):
        line = jnp.zeros((ROWS, 128), i32)
        for c in range(t, min(t + groups, nc)):
            diag = lane2 == slot2 + (c - t) * ROWS
            line = line + jnp.where(diag, columns[c], 0)
        line = fold(line[:8] + line[8:], 0, jnp.add)
        across.append(jnp.concatenate([line, line], axis=0))
        srow = jnp.where(sub == t // groups, line % 64, srow)
    table[pl.ds(8, 8), :] = srow

    span = min(128, width)
    for t, wide in enumerate(across):
        owner = lane2 // ROWS + t * groups
        weight = jnp.zeros((ROWS, 128), i32)
        for c in range(nc):
            weight = jnp.where(owner == c, coef_ref[c], weight)
        for c in range(nc):
            same = (columns[c] // 64 == wide // 64) & (wide > 0) & (owner != c)
            piece = jnp.where(same, weight, 0).astype(jnp.float32).astype(jnp.bfloat16)
            mix[pl.ds(c * ROWS, ROWS), pl.ds(t * 128, span)] = piece[:, :span]


def peak(values):
    m = functools.reduce(jnp.maximum, [jnp.abs(v) for v in values])
    if m.shape[0] > 8:
        m = jnp.maximum(m[:8], m[8:])
    return jnp.maximum(fold(m, 0, jnp.maximum)[0:1], 1e-30)


def code(a, b, inverse):
    qa = jnp.floor(a * inverse + 0.5).astype(jnp.int32)
    qb = jnp.floor(b * inverse + 0.5).astype(jnp.int32)
    return (qa << 16) | (qb & 0xFFFF)


def decode(word, unit):
    a = (word >> 16).astype(jnp.float32) * unit
    b = ((word << 16) >> 16).astype(jnp.float32) * unit
    return a, b


LEVELS = 32767.0


def stencil(cur, low, high, left, right, rates, masks):
    e_last, e_first, f_last, f_first, d_low, d_high = masks
    out = []
    down = [pltpu.roll(x, 32, 1) for x in cur]
    up = [pltpu.roll(x, 96, 1) for x in cur]
    for h in range(2):
        x = cur[h]
        pairs = [(high[h], low[h]), (right[h], left[h])]
        n = x.shape[0]
        pairs.append((pltpu.roll(x, n - 1, 0), pltpu.roll(x, 1, 0)))
        pairs.append(
            (jnp.where(d_high, up[1 - h], up[h]), jnp.where(d_low, down[1 - h], down[h]))
        )
        pairs.append(
            (
                jnp.where(e_last, pltpu.roll(x, 28, 1), pltpu.roll(x, 124, 1)),
                jnp.where(e_first, pltpu.roll(x, 100, 1), pltpu.roll(x, 4, 1)),
            )
        )
        pairs.append(
            (
                jnp.where(f_last, pltpu.roll(x, 3, 1), pltpu.roll(x, 127, 1)),
                jnp.where(f_first, pltpu.roll(x, 125, 1), pltpu.roll(x, 1, 1)),
            )
        )
        total = None
        drift = None
        for d, (fwd, bwd) in enumerate(pairs):
            s = fwd + bwd
            m = rates[h][d] * (fwd - bwd)
            total = s if total is None else total + s
            drift = m if drift is None else drift + m
        out.append(0.28 * x + 0.06 * total - 0.5 * drift)
    return out


def kernel(
    nc, nd,
    coef_ref, lists_ref, dens_ref, vel_ref,
    out_ref,
    ubuf, hs, hr, hs_unit, hr_unit, hdec, line, tsend, tall, eback, erecv, ez, osend,
    out_w, in_w, out2_w, in2_w, out_u, in_u, out2_u, in2_u, mix, padded, table, comb, tab,
    tab_sem, hs_sem, hr_sem, a_sem, b_sem,
):
    mc = lax.axis_index("comp")
    md = lax.axis_index("dom")
    nb = dens_ref.shape[1]
    chunks = min(CHUNKS, nb // 2)
    size = nb // chunks
    up_d = lax.rem(md + 1, nd)
    dn_d = lax.rem(md + nd - 1, nd)

    barrier = pltpu.get_barrier_semaphore()

    @pl.loop(1, nd)
    def _(i):
        pl.semaphore_signal(barrier, inc=1, device_id={"dom": lax.rem(md + i, nd)})

    @pl.loop(1, nc)
    def _(i):
        pl.semaphore_signal(barrier, inc=1, device_id={"comp": lax.rem(mc + i, nc)})

    def halo(step, way, ch):
        peer = {"dom": up_d if way == 0 else dn_d}
        return [
            pltpu.make_async_remote_copy(
                src_ref=src.at[step, way, ch],
                dst_ref=dst.at[step, way, ch],
                send_sem=hs_sem.at[kind, step, way, ch],
                recv_sem=hr_sem.at[kind, step, way, ch],
                device_id=peer,
            )
            for kind, (src, dst) in enumerate(((hs, hr), (hs_unit, hr_unit)))
        ]

    def half(h):
        return pl.ds(h * 128, 128)

    pair = size // 2

    def halo_send(src, step, ch):
        for way in range(2):
            for h in range(2):
                vals = [src[1 - way, ch * size + i, :, half(h)] for i in range(size)]
                top = peak(vals)
                inverse = LEVELS / top
                for i in range(pair):
                    hs[step, way, ch, i, :, half(h)] = code(vals[i], vals[i + pair], inverse)
                hs_unit[step, way, ch, pl.ds(h, 1), :] = top * (1.0 / LEVELS)
            for copy in halo(step, way, ch):
                copy.start()

    def halo_receive(step, ch):
        for way in range(2):
            for copy in halo(step, way, ch):
                copy.wait_recv()
            for h in range(2):
                unit = hr_unit[step, way, ch, pl.ds(h, 1), :]
                for i in range(pair):
                    first, second = decode(hr[step, way, ch, i, :, half(h)], unit)
                    hdec[way, ch * size + i, :, half(h)] = first
                    hdec[way, ch * size + i + pair, :, half(h)] = second

    pl.semaphore_wait(barrier, nd + nc - 2)

    @pl.loop(0, chunks)
    def _(ch):
        halo_send(dens_ref, 0, ch)

    ns = 2 * nd
    tables(lists_ref, coef_ref, padded, table, comb, mix, nc, ns)
    fetch = pltpu.make_async_copy(table, tab, tab_sem)
    fetch.start()

    per = 128 // ns

    def slot_of(s):
        return tab[mc // per, (mc % per) * ns + s]

    def slab_of(j):
        at = mc * ROWS + j
        return tab[8 + at // 128, at % 128]

    nrow = dens_ref.shape[2]
    lane = lax.broadcasted_iota(jnp.int32, (nrow, 128), 1)
    e_idx = (lane // E_STRIDE) % E_EXT
    f_idx = lane % F_EXT
    masks = (
        e_idx == E_EXT - 1, e_idx == 0, f_idx == F_EXT - 1, f_idx == 0,
        lane < 32, lane >= 96,
    )

    def halves(ref, *idx):
        return [ref[(*idx, slice(None), pl.ds(h * 128, 128))].astype(jnp.float32) for h in range(2)]

    for step in range(STEPS):
        src = dens_ref if step == 0 else ubuf.at[(step - 1) % 2]
        dst = ubuf.at[step % 2]

        @pl.loop(0, chunks)
        def _(ch):
            halo_receive(step, ch)

            @pl.loop(0, size)
            def _(i):
                b = ch * size + i
                bm = lax.rem(b + nb - 1, nb)
                bp = lax.rem(b + 1, nb)
                first = halves(src, 0, b)
                second = halves(src, 1, b)
                lo = halves(hdec, 0, b)
                hi = halves(hdec, 1, b)
                for p in range(2):
                    cur = first if p == 0 else second
                    rates = [
                        [
                            vel_ref[d, p, b, :, pl.ds(h * 128, 128)].astype(jnp.float32)
                            for d in range(6)
                        ]
                        for h in range(2)
                    ]
                    new = stencil(
                        cur,
                        lo if p == 0 else first,
                        second if p == 0 else hi,
                        halves(src, p, bm),
                        halves(src, p, bp),
                        rates,
                        masks,
                    )
                    for h in range(2):
                        dst[p, b, :, pl.ds(h * 128, 128)] = new[h]

            if step < STEPS - 1:
                halo_send(dst, step + 1, ch)

    last = ubuf.at[(STEPS - 1) % 2]

    def spread(refs, phase, axis, me, peer):
        return [
            pltpu.make_async_remote_copy(
                src_ref=src.at[peer],
                dst_ref=dst.at[me],
                send_sem=a_sem.at[phase, kind, peer],
                recv_sem=b_sem.at[phase, kind, me],
                device_id={axis: peer},
            )
            for kind, (src, dst) in enumerate(refs)
        ]

    def arrive(refs, phase, axis, me, peer):
        for kind, (src, dst) in enumerate(refs):
            pltpu.make_async_remote_copy(
                src_ref=src.at[peer],
                dst_ref=dst.at[peer],
                send_sem=a_sem.at[phase, kind, peer],
                recv_sem=b_sem.at[phase, kind, peer],
                device_id={axis: peer},
            ).wait_recv()

    def exchange_start(refs, phase, axis, me, n):
        @pl.loop(1, n)
        def _(i):
            for copy in spread(refs, phase, axis, me, lax.rem(me + i, n)):
                copy.start()

    def exchange_wait(refs, phase, axis, me, n):
        @pl.loop(1, n)
        def _(i):
            arrive(refs, phase, axis, me, lax.rem(me + n - i, n))

    def encode_planes(first, second, d, words, units):
        for h in range(2):
            x, y = first(h), second(h)
            top = peak([x, y])
            words[d, :, half(h)] = code(x, y, LEVELS / top)
            units[d, pl.ds(h, 1), :] = top * (1.0 / LEVELS)

    ph0 = (((out_w, in_w), (out_u, in_u)), 0, "dom")

    @pl.loop(1, nd)
    def _(i):
        d = lax.rem(md + i, nd)
        encode_planes(
            lambda h: last[0, d, :, half(h)], lambda h: last[1, d, :, half(h)], d, out_w, out_u
        )
        for copy in spread(*ph0, md, d):
            copy.start()

    for p in range(2):
        line[2 * md + p] = last[p, md]

    @pl.loop(1, nd)
    def _(i):
        d = lax.rem(md + nd - i, nd)
        arrive(*ph0, md, d)
        for h in range(2):
            x, y = decode(in_w[d, :, half(h)], in_u[d, pl.ds(h, 1), :])
            line[2 * d, :, half(h)] = x
            line[2 * d + 1, :, half(h)] = y

    fetch.wait()

    for part in range(2):
        rows = []
        for k in range(8):
            j = part * 8 + k
            if j >= USED:
                rows.append(jnp.zeros_like(line[0]))
                continue
            s = slab_of(j)
            h = s & (-s)
            w = jnp.where(s == 0, 0.0, 0.5)
            n = 2 * nd
            lo = (s - h) & (n - 1)
            hi = (s + h) & (n - 1)
            rows.append(line[s] - w * (line[lo] + line[hi]))
        block = jnp.stack(rows, axis=0)
        tsend[:, pl.ds(part * 8, 8), :] = jnp.swapaxes(block, 0, 1)

    ph1 = (((tsend, tall),), 1, "comp")
    exchange_start(*ph1, mc, nc)
    tall[mc] = tsend[mc]
    exchange_wait(*ph1, mc, nc)

    t = tall[...].reshape(nc * ROWS, 256)
    m = mix[...]
    acc = None
    for part in range(3):
        piece = t.astype(jnp.bfloat16)
        t = t - piece.astype(jnp.float32)
        prod = jnp.dot(m, piece, preferred_element_type=jnp.float32)
        acc = prod if acc is None else acc + prod
    eback[...] = acc.reshape(nc, ROWS, 256)

    ph2 = (((eback, erecv),), 2, "comp")
    exchange_start(*ph2, mc, nc)
    erecv[mc] = eback[mc]
    exchange_wait(*ph2, mc, nc)

    for part in range(2):
        ez[pl.ds(part * 8, 8)] = jnp.swapaxes(erecv[:, pl.ds(part * 8, 8), :], 0, 1)

    n = 2 * nd
    for q in range(4):
        if q % 2 * 8 >= nrow:
            continue
        r = (pl.ds(q % 2 * 8, min(8, nrow)), pl.ds(q // 2 * 128, 128))
        planes = {}
        planes[0] = ez[(slot_of(0), *r)]
        gap = n // 2
        while gap >= 1:
            for s in range(gap, n, 2 * gap):
                planes[s] = ez[(slot_of(s), *r)] + 0.5 * (
                    planes[(s - gap) % n] + planes[(s + gap) % n]
                )
            gap //= 2
        for s in range(n):
            osend[(s, *r)] = planes[s]

    ph3 = (((out2_w, in2_w), (out2_u, in2_u)), 3, "dom")

    @pl.loop(1, nd)
    def _(i):
        d = lax.rem(md + i, nd)
        encode_planes(
            lambda h: osend[2 * d, :, half(h)],
            lambda h: osend[2 * d + 1, :, half(h)],
            d, out2_w, out2_u,
        )
        for copy in spread(*ph3, md, d):
            copy.start()

    own = coef_ref[mc].astype(jnp.float32)

    for p in range(2):
        out_ref[p, md] = own * last[p, md] + osend[2 * md + p]

    @pl.loop(1, nd)
    def _(i):
        d = lax.rem(md + nd - i, nd)
        arrive(*ph3, md, d)
        for h in range(2):
            both = decode(in2_w[d, :, half(h)], in2_u[d, pl.ds(h, 1), :])
            for p in range(2):
                out_ref[p, d, :, half(h)] = own * last[p, d, :, half(h)] + both[p]

    @pl.loop(0, chunks)
    def _(ch):
        for step in range(STEPS):
            for copy in halo(step, 0, ch) + halo(step, 1, ch):
                copy.wait_send()

    for ph, me, k in ((ph0, md, nd), (ph1, mc, nc), (ph2, mc, nc), (ph3, md, nd)):
        @pl.loop(1, k)
        def _(i):
            for copy in spread(*ph, me, lax.rem(me + i, k)):
                copy.wait_send()


def local(density, velocity, coefficients, owner_lists):
    nc = lax.axis_size("comp")
    nd = lax.axis_size("dom")
    _, planes, nb, nrow, lanes = density.shape
    f32 = jnp.float32
    chunks = min(CHUNKS, nb // 2)
    smem = pl.BlockSpec(memory_space=pltpu.SMEM)
    vmem = pl.BlockSpec(memory_space=pltpu.VMEM)
    out = pl.pallas_call(
        functools.partial(kernel, nc, nd),
        out_shape=jax.ShapeDtypeStruct((planes, nb, nrow, lanes), f32),
        in_specs=[smem, vmem, vmem, vmem],
        out_specs=vmem,
        scratch_shapes=[
            pltpu.VMEM((2, planes, nb, nrow, lanes), f32),
            *[pltpu.VMEM((STEPS, 2, chunks, nb // chunks // 2, nrow, lanes), jnp.int32)] * 2,
            *[pltpu.VMEM((STEPS, 2, chunks, 2, 128), f32)] * 2,
            pltpu.VMEM((2, nb, nrow, lanes), f32),
            pltpu.VMEM((planes * nd, nrow, lanes), f32),
            pltpu.VMEM((nc, ROWS, lanes), f32),
            pltpu.VMEM((nc, ROWS, lanes), f32),
            pltpu.VMEM((nc, ROWS, lanes), f32),
            pltpu.VMEM((nc, ROWS, lanes), f32),
            pltpu.VMEM((ROWS, nrow, lanes), f32),
            pltpu.VMEM((planes * nd, nrow, lanes), f32),
            *[pltpu.VMEM((nd, nrow, lanes), jnp.int32)] * 4,
            *[pltpu.VMEM((nd, 2, 128), f32)] * 4,
            pltpu.VMEM((nc * ROWS, nc * ROWS), jnp.bfloat16),
            pltpu.VMEM((nc, pl.cdiv(owner_lists.shape[0], 128) * 128), jnp.int32),
            pltpu.VMEM((16, 128), jnp.int32),
            pltpu.VMEM((8, 128), jnp.int32),
            pltpu.SMEM((16, 128), jnp.int32),
            pltpu.SemaphoreType.DMA,
            pltpu.SemaphoreType.DMA((2, STEPS, 2, chunks)),
            pltpu.SemaphoreType.DMA((2, STEPS, 2, chunks)),
            pltpu.SemaphoreType.DMA((4, 2, max(nc, nd))),
            pltpu.SemaphoreType.DMA((4, 2, max(nc, nd))),
        ],
        compiler_params=pltpu.CompilerParams(collective_id=0, has_side_effects=True),
    )(coefficients, owner_lists.T, density[0], velocity[0])
    return out[None]


def solution(mesh):
    in_specs = (
        P("comp", "dom", None, None, None),
        P("comp", None, "dom", None, None, None),
        P(),
        P(),
    )
    out_specs = P("comp", "dom", None, None, None)
    return jax.shard_map(local, mesh=mesh, in_specs=in_specs, out_specs=out_specs, check_vma=False)
```

```python
import functools

import jax
import jax.numpy as jnp
import numpy as np
from jax import lax
from jax.experimental import pallas as pl
from jax.experimental.pallas import tpu as pltpu
from jax.sharding import PartitionSpec as P

STEPS = 4
E_STRIDE, E_EXT = 4, 8
F_STRIDE, F_EXT = 1, 4
ROWS = 16
HALF = 6
ZERO = 16
CHUNKS = 4


def fold(x, axis, op):
    shift = x.shape[axis] // 2
    while shift:
        x = op(x, pltpu.roll(x, shift, axis))
        shift //= 2
    return x


def tables(lists_ref, coef_ref, padded, table, comb, mix, nc, ns):
    i32 = jnp.int32
    depth, blocks = lists_ref.shape
    lane = lax.broadcasted_iota(i32, (8, 128), 1)
    sub = lax.broadcasted_iota(i32, (8, 128), 0)
    tiles = max(1, nc * ns // 128)
    per = 128 // ns
    total = nc * ns

    padded[...] = jnp.full(padded.shape, -1, i32)
    padded[:, pl.ds(0, blocks)] = lists_ref[...]
    slab = lax.broadcasted_iota(i32, (total, 128), 0)
    wide = lax.broadcasted_iota(i32, (total, 128), 1)
    number = jnp.zeros((total, 128), i32)
    for t in range(padded.shape[1] // 128):
        rows = padded[:, pl.ds(t * 128, 128)]
        own = jnp.broadcast_to(rows[:, None, :], (nc, ns, 128)).reshape(total, 128)
        found = (rows[0:1] == slab) | (rows[1:2] == slab) | (own == slab)
        found = found & (rows[1:2] >= 0)
        number = jnp.maximum(number, jnp.where(found, wide + (t * 128 + 1), 0))
    number = fold(number, 1, jnp.maximum)
    number = jnp.where(wide == slab % 128, number, 0)

    ident = jnp.zeros((8, 128), i32)
    for r in range(tiles):
        part = number[r * 128 : min(r * 128 + 128, total)]
        part = jnp.sum(part.reshape(-1, 8, 128), axis=0)
        ident = jnp.where(sub == r, fold(part, 0, jnp.add), ident)
    place = lane % ns
    one = jnp.where(ident > 0, 1, 0)
    count = one
    shift = 1
    while shift < ns:
        count = count + jnp.where(place >= shift, pltpu.roll(count, shift, 1), 0)
        shift *= 2
    slot = count - 1 + jnp.where(count > HALF, 8 - HALF, 0)
    slot = jnp.where(ident > 0, slot, ZERO)
    table[pl.ds(0, 8), :] = slot
    both = jnp.where(ident > 0, ident * 64 + place, 0)
    comb[pl.ds(0, 8), :] = both

    lane2 = lax.broadcasted_iota(i32, (ROWS, 128), 1)
    slot2 = lax.broadcasted_iota(i32, (ROWS, 128), 0)
    columns = []
    for c in range(nc):
        r = c // per
        row = jnp.broadcast_to(table[pl.ds(r, 1), :], (ROWS, 128))
        val = jnp.broadcast_to(comb[pl.ds(r, 1), :], (ROWS, 128))
        mine = (row == slot2) & (lane2 // ns == c % per)
        columns.append(fold(jnp.where(mine, val, 0), 1, jnp.add))

    groups = 128 // ROWS
    width = nc * ROWS
    srow = jnp.zeros((8, 128), i32)
    across = []
    for t in range(0, nc, groups):
        line = jnp.zeros((ROWS, 128), i32)
        for c in range(t, min(t + groups, nc)):
            diag = lane2 == slot2 + (c - t) * ROWS
            line = line + jnp.where(diag, columns[c], 0)
        line = fold(line[:8] + line[8:], 0, jnp.add)
        across.append(jnp.concatenate([line, line], axis=0))
        srow = jnp.where(sub == t // groups, line % 64, srow)
    table[pl.ds(8, 8), :] = srow

    span = min(128, width)
    for t, wide in enumerate(across):
        owner = lane2 // ROWS + t * groups
        weight = jnp.zeros((ROWS, 128), i32)
        for c in range(nc):
            weight = jnp.where(owner == c, coef_ref[c], weight)
        for c in range(nc):
            same = (columns[c] // 64 == wide // 64) & (wide > 0) & (owner != c)
            piece = jnp.where(same, weight, 0).astype(jnp.float32).astype(jnp.bfloat16)
            mix[pl.ds(c * ROWS, ROWS), pl.ds(t * 128, span)] = piece[:, :span]


def peak(values):
    m = functools.reduce(jnp.maximum, [jnp.abs(v) for v in values])
    if m.shape[0] > 8:
        m = jnp.maximum(m[:8], m[8:])
    return jnp.maximum(fold(m, 0, jnp.maximum)[0:1], 1e-30)


def code(a, b, inverse):
    qa = jnp.floor(a * inverse + 0.5).astype(jnp.int32)
    qb = jnp.floor(b * inverse + 0.5).astype(jnp.int32)
    return (qa << 16) | (qb & 0xFFFF)


def decode(word, unit):
    a = (word >> 16).astype(jnp.float32) * unit
    b = ((word << 16) >> 16).astype(jnp.float32) * unit
    return a, b


LEVELS = 32767.0
FINE = 4096.0


def exponent(top):
    return jnp.ceil(jnp.log2(top) * FINE).astype(jnp.int32) + 1


def scale(e, sign):
    power = jnp.exp2(e.astype(jnp.float32) * (sign / FINE))
    return power * (1.0 / 32700.0) if sign > 0 else power * 32700.0


def stencil(cur, low, high, left, right, rates, masks):
    e_last, e_first, f_last, f_first, d_low, d_high = masks
    out = []
    down = [pltpu.roll(x, 32, 1) for x in cur]
    up = [pltpu.roll(x, 96, 1) for x in cur]
    for h in range(2):
        x = cur[h]
        pairs = [(high[h], low[h]), (right[h], left[h])]
        n = x.shape[0]
        pairs.append((pltpu.roll(x, n - 1, 0), pltpu.roll(x, 1, 0)))
        pairs.append(
            (jnp.where(d_high, up[1 - h], up[h]), jnp.where(d_low, down[1 - h], down[h]))
        )
        pairs.append(
            (
                jnp.where(e_last, pltpu.roll(x, 28, 1), pltpu.roll(x, 124, 1)),
                jnp.where(e_first, pltpu.roll(x, 100, 1), pltpu.roll(x, 4, 1)),
            )
        )
        pairs.append(
            (
                jnp.where(f_last, pltpu.roll(x, 3, 1), pltpu.roll(x, 127, 1)),
                jnp.where(f_first, pltpu.roll(x, 125, 1), pltpu.roll(x, 1, 1)),
            )
        )
        total = None
        drift = None
        for d, (fwd, bwd) in enumerate(pairs):
            s = fwd + bwd
            m = rates[h][d] * (fwd - bwd)
            total = s if total is None else total + s
            drift = m if drift is None else drift + m
        out.append(0.28 * x + 0.06 * total - 0.5 * drift)
    return out


def kernel(
    nc, nd,
    coef_ref, lists_ref, dens_ref, vel_ref,
    out_ref,
    ubuf, hs, hr, hs_unit, hr_unit, hdec, line, tsend, tall, eback, erecv, ez, osend,
    out_w, in_w, out2_w, in2_w, out_u, in_u, out2_u, in2_u, mix, padded, table, comb, tab,
    tab_sem, hs_sem, hr_sem, a_sem, b_sem,
):
    mc = lax.axis_index("comp")
    md = lax.axis_index("dom")
    nb = dens_ref.shape[1]
    chunks = min(CHUNKS, nb // 2)
    size = nb // chunks
    up_d = lax.rem(md + 1, nd)
    dn_d = lax.rem(md + nd - 1, nd)

    barrier = pltpu.get_barrier_semaphore()

    @pl.loop(1, nd)
    def _(i):
        pl.semaphore_signal(barrier, inc=1, device_id={"dom": lax.rem(md + i, nd)})

    @pl.loop(1, nc)
    def _(i):
        pl.semaphore_signal(barrier, inc=1, device_id={"comp": lax.rem(mc + i, nc)})

    def halo(step, way, ch):
        peer = {"dom": up_d if way == 0 else dn_d}
        return [
            pltpu.make_async_remote_copy(
                src_ref=src.at[step, way, ch],
                dst_ref=dst.at[step, way, ch],
                send_sem=hs_sem.at[kind, step, way, ch],
                recv_sem=hr_sem.at[kind, step, way, ch],
                device_id=peer,
            )
            for kind, (src, dst) in enumerate(((hs, hr), (hs_unit, hr_unit)))
        ]

    def half(h):
        return pl.ds(h * 128, 128)

    pair = size // 2

    def halo_send(src, step, ch):
        for way in range(2):
            for h in range(2):
                vals = [src[1 - way, ch * size + i, :, half(h)] for i in range(size)]
                top = peak(vals)
                inverse = LEVELS / top
                for i in range(pair):
                    hs[step, way, ch, i, :, half(h)] = code(vals[i], vals[i + pair], inverse)
                hs_unit[step, way, ch, pl.ds(h, 1), :] = top * (1.0 / LEVELS)
            for copy in halo(step, way, ch):
                copy.start()

    def halo_receive(step, ch):
        for way in range(2):
            for copy in halo(step, way, ch):
                copy.wait_recv()
            for h in range(2):
                unit = hr_unit[step, way, ch, pl.ds(h, 1), :]
                for i in range(pair):
                    first, second = decode(hr[step, way, ch, i, :, half(h)], unit)
                    hdec[way, ch * size + i, :, half(h)] = first
                    hdec[way, ch * size + i + pair, :, half(h)] = second

    pl.semaphore_wait(barrier, nd + nc - 2)

    @pl.loop(0, chunks)
    def _(ch):
        halo_send(dens_ref, 0, ch)

    ns = 2 * nd
    tables(lists_ref, coef_ref, padded, table, comb, mix, nc, ns)
    fetch = pltpu.make_async_copy(table, tab, tab_sem)
    fetch.start()

    per = 128 // ns

    def slot_of(s):
        return tab[mc // per, (mc % per) * ns + s]

    def slab_of(j):
        at = mc * ROWS + j
        return tab[8 + at // 128, at % 128]

    nrow = dens_ref.shape[2]
    lane = lax.broadcasted_iota(jnp.int32, (nrow, 128), 1)
    e_idx = (lane // E_STRIDE) % E_EXT
    f_idx = lane % F_EXT
    masks = (
        e_idx == E_EXT - 1, e_idx == 0, f_idx == F_EXT - 1, f_idx == 0,
        lane < 32, lane >= 96,
    )

    def halves(ref, *idx):
        return [ref[(*idx, slice(None), pl.ds(h * 128, 128))].astype(jnp.float32) for h in range(2)]

    for step in range(STEPS):
        src = dens_ref if step == 0 else ubuf.at[(step - 1) % 2]
        dst = ubuf.at[step % 2]

        @pl.loop(0, chunks)
        def _(ch):
            halo_receive(step, ch)

            @pl.loop(0, size)
            def _(i):
                b = ch * size + i
                bm = lax.rem(b + nb - 1, nb)
                bp = lax.rem(b + 1, nb)
                first = halves(src, 0, b)
                second = halves(src, 1, b)
                lo = halves(hdec, 0, b)
                hi = halves(hdec, 1, b)
                for p in range(2):
                    cur = first if p == 0 else second
                    rates = [
                        [
                            vel_ref[d, p, b, :, pl.ds(h * 128, 128)].astype(jnp.float32)
                            for d in range(6)
                        ]
                        for h in range(2)
                    ]
                    new = stencil(
                        cur,
                        lo if p == 0 else first,
                        second if p == 0 else hi,
                        halves(src, p, bm),
                        halves(src, p, bp),
                        rates,
                        masks,
                    )
                    for h in range(2):
                        dst[p, b, :, pl.ds(h * 128, 128)] = new[h]

            if step < STEPS - 1:
                halo_send(dst, step + 1, ch)

    last = ubuf.at[(STEPS - 1) % 2]

    def spread(refs, phase, axis, me, peer):
        return [
            pltpu.make_async_remote_copy(
                src_ref=src.at[peer],
                dst_ref=dst.at[me],
                send_sem=a_sem.at[phase, kind, peer],
                recv_sem=b_sem.at[phase, kind, me],
                device_id={axis: peer},
            )
            for kind, (src, dst) in enumerate(refs)
        ]

    def arrive(refs, phase, axis, me, peer):
        for kind, (src, dst) in enumerate(refs):
            pltpu.make_async_remote_copy(
                src_ref=src.at[peer],
                dst_ref=dst.at[peer],
                send_sem=a_sem.at[phase, kind, peer],
                recv_sem=b_sem.at[phase, kind, peer],
                device_id={axis: peer},
            ).wait_recv()

    nz, nx = nd // 2, nc // 4

    def swing(k, n):
        return n // 2 + k // 2 - (k % 2) * k

    def dom_peer(i, sign):
        z = lax.rem(md % nz + sign * swing(i // 2, nz) + nz, nz)
        y = lax.rem(md // nz + 1 - i % 2, 2)
        return y * nz + z

    def comp_peer(i, sign):
        q = i // 2
        x = lax.rem(mc // 4 + sign * swing(q % nx, nx) + nx, nx)
        y = lax.rem((mc // 2) % 2 + 1 - q // nx, 2)
        core = lax.rem(mc % 2 + 1 - i % 2, 2)
        return (x * 2 + y) * 2 + core

    def exchange_start(refs, phase, axis, me, n):
        @pl.loop(0, n - 1)
        def _(i):
            for copy in spread(refs, phase, axis, me, comp_peer(i, 1)):
                copy.start()

    def exchange_wait(refs, phase, axis, me, n):
        @pl.loop(0, n - 1)
        def _(i):
            arrive(refs, phase, axis, me, comp_peer(i, -1))

    def encode_planes(first, second, d, words, units):
        for h in range(2):
            x, y = first(h), second(h)
            top = peak([x, y])
            words[d, :, half(h)] = code(x, y, LEVELS / top)
            units[d, pl.ds(h, 1), :] = top * (1.0 / LEVELS)

    ph0 = (((out_w, in_w), (out_u, in_u)), 0, "dom")

    @pl.loop(0, nd - 1)
    def _(i):
        d = dom_peer(i, 1)
        encode_planes(
            lambda h: last[0, d, :, half(h)], lambda h: last[1, d, :, half(h)], d, out_w, out_u
        )
        for copy in spread(*ph0, md, d):
            copy.start()

    for p in range(2):
        line[2 * md + p] = last[p, md]

    @pl.loop(0, nd - 1)
    def _(i):
        d = dom_peer(i, -1)
        arrive(*ph0, md, d)
        for h in range(2):
            x, y = decode(in_w[d, :, half(h)], in_u[d, pl.ds(h, 1), :])
            line[2 * d, :, half(h)] = x
            line[2 * d + 1, :, half(h)] = y

    fetch.wait()

    for h in range(2):
        tops = []
        for k in range(HALF):
            for j in (k, k + 8):
                s = slab_of(j)
                g = s & (-s)
                w = jnp.where(s == 0, 0.0, 0.5)
                low, up = (s - g) & (ns - 1), (s + g) & (ns - 1)
                t = line[s, :, half(h)] - w * (line[low, :, half(h)] + line[up, :, half(h)])
                tops.append(t)
        top = functools.reduce(jnp.maximum, [jnp.abs(t) for t in tops])
        e = exponent(jnp.maximum(top, 1e-30))
        inverse = scale(e, -1)
        words = [code(tops[2 * k], tops[2 * k + 1], inverse) for k in range(HALF)]
        block = jnp.stack(words + [e, jnp.zeros_like(e)], axis=0)
        tsend[:, :, half(h)] = jnp.swapaxes(block, 0, 1)

    ph1 = (((tsend, tall),), 1, "comp")
    exchange_start(*ph1, mc, nc)
    tall[mc] = tsend[mc]
    exchange_wait(*ph1, mc, nc)

    blocks = []
    for c in range(nc):
        blocks.extend(decode(tall[c], scale(tall[c, pl.ds(HALF, 1), :], 1)))
    t = jnp.concatenate(blocks, axis=0)
    m = mix[...]
    acc = None
    for part in range(2):
        piece = t.astype(jnp.bfloat16)
        t = t - piece.astype(jnp.float32)
        prod = jnp.dot(m, piece, preferred_element_type=jnp.float32)
        acc = prod if acc is None else acc + prod
    mark = lax.broadcasted_iota(jnp.int32, (8, 256), 0) == HALF
    for c in range(nc):
        x = acc[c * ROWS : c * ROWS + 8]
        y = acc[c * ROWS + 8 : c * ROWS + 16]
        top = fold(jnp.maximum(jnp.abs(x), jnp.abs(y)), 0, jnp.maximum)
        e = exponent(jnp.maximum(top, 1e-30))
        eback[c] = jnp.where(mark, e, code(x, y, scale(e, -1)))

    ph2 = (((eback, erecv),), 2, "comp")
    exchange_start(*ph2, mc, nc)
    erecv[mc] = eback[mc]
    exchange_wait(*ph2, mc, nc)

    for h in range(2):
        words = jnp.swapaxes(erecv[:, :, half(h)], 0, 1)
        unit = scale(words[HALF], 1)
        for k in range(HALF):
            x, y = decode(words[k], unit)
            ez[k, :, half(h)] = x
            ez[k + 8, :, half(h)] = y
    ez[ZERO] = jnp.zeros(ez.shape[1:], jnp.float32)

    n = 2 * nd
    for q in range(4):
        if q % 2 * 8 >= nrow:
            continue
        r = (pl.ds(q % 2 * 8, min(8, nrow)), pl.ds(q // 2 * 128, 128))
        planes = {}
        planes[0] = ez[(slot_of(0), *r)]
        gap = n // 2
        while gap >= 1:
            for s in range(gap, n, 2 * gap):
                planes[s] = ez[(slot_of(s), *r)] + 0.5 * (
                    planes[(s - gap) % n] + planes[(s + gap) % n]
                )
            gap //= 2
        for s in range(n):
            osend[(s, *r)] = planes[s]

    ph3 = (((out2_w, in2_w), (out2_u, in2_u)), 3, "dom")

    @pl.loop(0, nd - 1)
    def _(i):
        d = dom_peer(i, 1)
        encode_planes(
            lambda h: osend[2 * d, :, half(h)],
            lambda h: osend[2 * d + 1, :, half(h)],
            d, out2_w, out2_u,
        )
        for copy in spread(*ph3, md, d):
            copy.start()

    own = coef_ref[mc].astype(jnp.float32)

    for p in range(2):
        out_ref[p, md] = own * last[p, md] + osend[2 * md + p]

    @pl.loop(0, nd - 1)
    def _(i):
        d = dom_peer(i, -1)
        arrive(*ph3, md, d)
        for h in range(2):
            both = decode(in2_w[d, :, half(h)], in2_u[d, pl.ds(h, 1), :])
            for p in range(2):
                out_ref[p, d, :, half(h)] = own * last[p, d, :, half(h)] + both[p]

    @pl.loop(0, chunks)
    def _(ch):
        for step in range(STEPS):
            for copy in halo(step, 0, ch) + halo(step, 1, ch):
                copy.wait_send()

    for ph, me, k in ((ph0, md, nd), (ph1, mc, nc), (ph2, mc, nc), (ph3, md, nd)):
        @pl.loop(1, k)
        def _(i):
            for copy in spread(*ph, me, lax.rem(me + i, k)):
                copy.wait_send()


def local(density, velocity, coefficients, owner_lists):
    nc = lax.axis_size("comp")
    nd = lax.axis_size("dom")
    _, planes, nb, nrow, lanes = density.shape
    f32 = jnp.float32
    chunks = min(CHUNKS, nb // 2)
    smem = pl.BlockSpec(memory_space=pltpu.SMEM)
    vmem = pl.BlockSpec(memory_space=pltpu.VMEM)
    out = pl.pallas_call(
        functools.partial(kernel, nc, nd),
        out_shape=jax.ShapeDtypeStruct((planes, nb, nrow, lanes), f32),
        in_specs=[smem, vmem, vmem, vmem],
        out_specs=vmem,
        scratch_shapes=[
            pltpu.VMEM((2, planes, nb, nrow, lanes), f32),
            *[pltpu.VMEM((STEPS, 2, chunks, nb // chunks // 2, nrow, lanes), jnp.int32)] * 2,
            *[pltpu.VMEM((STEPS, 2, chunks, 2, 128), f32)] * 2,
            pltpu.VMEM((2, nb, nrow, lanes), f32),
            pltpu.VMEM((planes * nd, nrow, lanes), f32),
            *[pltpu.VMEM((nc, 8, lanes), jnp.int32)] * 4,
            pltpu.VMEM((ZERO + 1, nrow, lanes), f32),
            pltpu.VMEM((planes * nd, nrow, lanes), f32),
            *[pltpu.VMEM((nd, nrow, lanes), jnp.int32)] * 4,
            *[pltpu.VMEM((nd, 2, 128), f32)] * 4,
            pltpu.VMEM((nc * ROWS, nc * ROWS), jnp.bfloat16),
            pltpu.VMEM((nc, pl.cdiv(owner_lists.shape[0], 128) * 128), jnp.int32),
            pltpu.VMEM((16, 128), jnp.int32),
            pltpu.VMEM((8, 128), jnp.int32),
            pltpu.SMEM((16, 128), jnp.int32),
            pltpu.SemaphoreType.DMA,
            pltpu.SemaphoreType.DMA((2, STEPS, 2, chunks)),
            pltpu.SemaphoreType.DMA((2, STEPS, 2, chunks)),
            pltpu.SemaphoreType.DMA((4, 2, max(nc, nd))),
            pltpu.SemaphoreType.DMA((4, 2, max(nc, nd))),
        ],
        compiler_params=pltpu.CompilerParams(collective_id=0, has_side_effects=True),
    )(coefficients, owner_lists.T, density[0], velocity[0])
    return out[None]


def solution(mesh):
    in_specs = (
        P("comp", "dom", None, None, None),
        P("comp", None, "dom", None, None, None),
        P(),
        P(),
    )
    out_specs = P("comp", "dom", None, None, None)
    return jax.shard_map(local, mesh=mesh, in_specs=in_specs, out_specs=out_specs, check_vma=False)
```

```python
import functools

import jax
import jax.numpy as jnp
import numpy as np
from jax import lax
from jax.experimental import pallas as pl
from jax.experimental.pallas import tpu as pltpu
from jax.sharding import PartitionSpec as P

STEPS = 4
E_STRIDE, E_EXT = 4, 8
F_STRIDE, F_EXT = 1, 4
ROWS = 16
HALF = 6
ZERO = 16
CHUNKS = 4


def fold(x, axis, op):
    shift = x.shape[axis] // 2
    while shift:
        x = op(x, pltpu.roll(x, shift, axis))
        shift //= 2
    return x


def tables(lists_ref, coef_ref, padded, table, comb, mix, nc, ns):
    i32 = jnp.int32
    depth, blocks = lists_ref.shape
    lane = lax.broadcasted_iota(i32, (8, 128), 1)
    sub = lax.broadcasted_iota(i32, (8, 128), 0)
    tiles = max(1, nc * ns // 128)
    per = 128 // ns
    total = nc * ns

    padded[...] = jnp.full(padded.shape, -1, i32)
    padded[:, pl.ds(0, blocks)] = lists_ref[...]
    slab = lax.broadcasted_iota(i32, (total, 128), 0)
    wide = lax.broadcasted_iota(i32, (total, 128), 1)
    number = jnp.zeros((total, 128), i32)
    for t in range(padded.shape[1] // 128):
        rows = padded[:, pl.ds(t * 128, 128)]
        own = jnp.broadcast_to(rows[:, None, :], (nc, ns, 128)).reshape(total, 128)
        found = (rows[0:1] == slab) | (rows[1:2] == slab) | (own == slab)
        found = found & (rows[1:2] >= 0)
        number = jnp.maximum(number, jnp.where(found, wide + (t * 128 + 1), 0))
    number = fold(number, 1, jnp.maximum)
    number = jnp.where(wide == slab % 128, number, 0)

    ident = jnp.zeros((8, 128), i32)
    for r in range(tiles):
        part = number[r * 128 : min(r * 128 + 128, total)]
        part = jnp.sum(part.reshape(-1, 8, 128), axis=0)
        ident = jnp.where(sub == r, fold(part, 0, jnp.add), ident)
    place = lane % ns
    one = jnp.where(ident > 0, 1, 0)
    count = one
    shift = 1
    while shift < ns:
        count = count + jnp.where(place >= shift, pltpu.roll(count, shift, 1), 0)
        shift *= 2
    slot = count - 1 + jnp.where(count > HALF, 8 - HALF, 0)
    slot = jnp.where(ident > 0, slot, ZERO)
    table[pl.ds(0, 8), :] = slot
    both = jnp.where(ident > 0, ident * 64 + place, 0)
    comb[pl.ds(0, 8), :] = both

    lane2 = lax.broadcasted_iota(i32, (ROWS, 128), 1)
    slot2 = lax.broadcasted_iota(i32, (ROWS, 128), 0)
    columns = []
    for c in range(nc):
        r = c // per
        row = jnp.broadcast_to(table[pl.ds(r, 1), :], (ROWS, 128))
        val = jnp.broadcast_to(comb[pl.ds(r, 1), :], (ROWS, 128))
        mine = (row == slot2) & (lane2 // ns == c % per)
        columns.append(fold(jnp.where(mine, val, 0), 1, jnp.add))

    groups = 128 // ROWS
    width = nc * ROWS
    srow = jnp.zeros((8, 128), i32)
    across = []
    for t in range(0, nc, groups):
        line = jnp.zeros((ROWS, 128), i32)
        for c in range(t, min(t + groups, nc)):
            diag = lane2 == slot2 + (c - t) * ROWS
            line = line + jnp.where(diag, columns[c], 0)
        line = fold(line[:8] + line[8:], 0, jnp.add)
        across.append(jnp.concatenate([line, line], axis=0))
        srow = jnp.where(sub == t // groups, line % 64, srow)
    table[pl.ds(8, 8), :] = srow

    span = min(128, width)
    for t, wide in enumerate(across):
        owner = lane2 // ROWS + t * groups
        weight = jnp.zeros((ROWS, 128), i32)
        for c in range(nc):
            weight = jnp.where(owner == c, coef_ref[c], weight)
        for c in range(nc):
            same = (columns[c] // 64 == wide // 64) & (wide > 0) & (owner != c)
            piece = jnp.where(same, weight, 0).astype(jnp.float32).astype(jnp.bfloat16)
            mix[pl.ds(c * ROWS, ROWS), pl.ds(t * 128, span)] = piece[:, :span]


def peak(values):
    m = functools.reduce(jnp.maximum, [jnp.abs(v) for v in values])
    if m.shape[0] > 8:
        m = jnp.maximum(m[:8], m[8:])
    return jnp.maximum(fold(m, 0, jnp.maximum)[0:1], 1e-30)


def code(a, b, inverse):
    qa = jnp.floor(a * inverse + 0.5).astype(jnp.int32)
    qb = jnp.floor(b * inverse + 0.5).astype(jnp.int32)
    return (qa << 16) | (qb & 0xFFFF)


def decode(word, unit):
    a = (word >> 16).astype(jnp.float32) * unit
    b = ((word << 16) >> 16).astype(jnp.float32) * unit
    return a, b


LEVELS = 32767.0
FINE = 4096.0


def exponent(top):
    return jnp.ceil(jnp.log2(top) * FINE).astype(jnp.int32) + 1


def scale(e, sign):
    power = jnp.exp2(e.astype(jnp.float32) * (sign / FINE))
    return power * (1.0 / 32700.0) if sign > 0 else power * 32700.0


def stencil(cur, beside, sign, left, right, rates, masks):
    e_last, e_first, f_last, f_first, d_low, d_high = masks
    out = []
    down = [pltpu.roll(x, 32, 1) for x in cur]
    up = [pltpu.roll(x, 96, 1) for x in cur]
    for h in range(2):
        x = cur[h]
        pairs = [(right[h], left[h])]
        n = x.shape[0]
        pairs.append((pltpu.roll(x, n - 1, 0), pltpu.roll(x, 1, 0)))
        pairs.append(
            (jnp.where(d_high, up[1 - h], up[h]), jnp.where(d_low, down[1 - h], down[h]))
        )
        pairs.append(
            (
                jnp.where(e_last, pltpu.roll(x, 28, 1), pltpu.roll(x, 124, 1)),
                jnp.where(e_first, pltpu.roll(x, 100, 1), pltpu.roll(x, 4, 1)),
            )
        )
        pairs.append(
            (
                jnp.where(f_last, pltpu.roll(x, 3, 1), pltpu.roll(x, 127, 1)),
                jnp.where(f_first, pltpu.roll(x, 125, 1), pltpu.roll(x, 1, 1)),
            )
        )
        total = None
        drift = None
        for d, (fwd, bwd) in enumerate(pairs):
            s = fwd + bwd
            m = rates[h][d + 1] * (fwd - bwd)
            total = s if total is None else total + s
            drift = m if drift is None else drift + m
        near = (0.06 - sign * 0.5 * rates[h][0]) * beside[h]
        out.append(0.28 * x + near + 0.06 * total - 0.5 * drift)
    return out


def kernel(
    nc, nd,
    coef_ref, lists_ref, dens_ref, vel_ref,
    out_ref,
    ubuf, hs, hr, hs_unit, hr_unit, base, line, tsend, tall, eback, erecv, ez, osend,
    out_w, in_w, out2_w, in2_w, out_u, in_u, out2_u, in2_u, mix, padded, table, comb, tab,
    tab_sem, hs_sem, hr_sem, a_sem, b_sem,
):
    mc = lax.axis_index("comp")
    md = lax.axis_index("dom")
    nb = dens_ref.shape[1]
    chunks = min(CHUNKS, nb // 2)
    size = nb // chunks
    up_d = lax.rem(md + 1, nd)
    dn_d = lax.rem(md + nd - 1, nd)

    barrier = pltpu.get_barrier_semaphore()

    @pl.loop(1, nd)
    def _(i):
        pl.semaphore_signal(barrier, inc=1, device_id={"dom": lax.rem(md + i, nd)})

    @pl.loop(1, nc)
    def _(i):
        pl.semaphore_signal(barrier, inc=1, device_id={"comp": lax.rem(mc + i, nc)})

    def halo(step, way, ch):
        peer = {"dom": up_d if way == 0 else dn_d}
        return [
            pltpu.make_async_remote_copy(
                src_ref=src.at[step, way, ch],
                dst_ref=dst.at[step, way, ch],
                send_sem=hs_sem.at[kind, step, way, ch],
                recv_sem=hr_sem.at[kind, step, way, ch],
                device_id=peer,
            )
            for kind, (src, dst) in enumerate(((hs, hr), (hs_unit, hr_unit)))
        ]

    def half(h):
        return pl.ds(h * 128, 128)

    pair = size // 2

    def halo_send(step, way, ch, values):
        for h in range(2):
            vals = values[h]
            top = peak(vals)
            inverse = LEVELS / top
            for i in range(pair):
                hs[step, way, ch, i, :, half(h)] = code(vals[i], vals[i + pair], inverse)
            hs_unit[step, way, ch, pl.ds(h, 1), :] = top * (1.0 / LEVELS)
        for copy in halo(step, way, ch):
            copy.start()

    def halo_receive(step, way, ch):
        for copy in halo(step, way, ch):
            copy.wait_recv()
        out = []
        for h in range(2):
            unit = hr_unit[step, way, ch, pl.ds(h, 1), :]
            both = [decode(hr[step, way, ch, i, :, half(h)], unit) for i in range(pair)]
            out.append([x for x, _ in both] + [y for _, y in both])
        return out

    pl.semaphore_wait(barrier, nd + nc - 2)

    @pl.loop(0, chunks)
    def _(ch):
        for way in range(2):
            halo_send(
                0, way, ch,
                [
                    [dens_ref[1 - way, ch + chunks * i, :, half(h)] for i in range(size)]
                    for h in range(2)
                ],
            )

    ns = 2 * nd
    tables(lists_ref, coef_ref, padded, table, comb, mix, nc, ns)
    fetch = pltpu.make_async_copy(table, tab, tab_sem)
    fetch.start()

    per = 128 // ns

    def slot_of(s):
        return tab[mc // per, (mc % per) * ns + s]

    def slab_of(j):
        at = mc * ROWS + j
        return tab[8 + at // 128, at % 128]

    nrow = dens_ref.shape[2]
    lane = lax.broadcasted_iota(jnp.int32, (nrow, 128), 1)
    e_idx = (lane // E_STRIDE) % E_EXT
    f_idx = lane % F_EXT
    masks = (
        e_idx == E_EXT - 1, e_idx == 0, f_idx == F_EXT - 1, f_idx == 0,
        lane < 32, lane >= 96,
    )

    def halves(ref, *idx):
        return [ref[(*idx, slice(None), pl.ds(h * 128, 128))].astype(jnp.float32) for h in range(2)]

    last = ubuf.at[(STEPS - 1) % 2]

    def spread(refs, phase, axis, me, peer):
        return [
            pltpu.make_async_remote_copy(
                src_ref=src.at[peer],
                dst_ref=dst.at[me],
                send_sem=a_sem.at[phase, kind, peer],
                recv_sem=b_sem.at[phase, kind, me],
                device_id={axis: peer},
            )
            for kind, (src, dst) in enumerate(refs)
        ]

    def arrive(refs, phase, axis, me, peer):
        for kind, (src, dst) in enumerate(refs):
            pltpu.make_async_remote_copy(
                src_ref=src.at[peer],
                dst_ref=dst.at[peer],
                send_sem=a_sem.at[phase, kind, peer],
                recv_sem=b_sem.at[phase, kind, peer],
                device_id={axis: peer},
            ).wait_recv()

    nz, nx = nd // 2, nc // 4

    def swing(k, n):
        return n // 2 + k // 2 - (k % 2) * k

    def dom_peer(i, sign):
        z = lax.rem(md % nz + sign * swing(i // 2, nz) + nz, nz)
        y = lax.rem(md // nz + 1 - i % 2, 2)
        return y * nz + z

    def comp_peer(i, sign):
        q = i // 2
        x = lax.rem(mc // 4 + sign * swing(q % nx, nx) + nx, nx)
        y = lax.rem((mc // 2) % 2 + 1 - q // nx, 2)
        core = lax.rem(mc % 2 + 1 - i % 2, 2)
        return (x * 2 + y) * 2 + core

    def exchange_start(refs, phase, axis, me, n):
        @pl.loop(0, n - 1)
        def _(i):
            for copy in spread(refs, phase, axis, me, comp_peer(i, 1)):
                copy.start()

    def exchange_wait(refs, phase, axis, me, n):
        @pl.loop(0, n - 1)
        def _(i):
            arrive(refs, phase, axis, me, comp_peer(i, -1))

    def encode_planes(first, second, d, words, units):
        for h in range(2):
            x, y = first(h), second(h)
            top = peak([x, y])
            words[d, :, half(h)] = code(x, y, LEVELS / top)
            units[d, pl.ds(h, 1), :] = top * (1.0 / LEVELS)

    ph0 = (((out_w, in_w), (out_u, in_u)), 0, "dom")

    for step in range(STEPS):
        src = dens_ref if step == 0 else ubuf.at[(step - 1) % 2]
        dst = ubuf.at[step % 2]

        @pl.loop(0, nb)
        def _(b):
            bm = lax.rem(b + nb - 1, nb)
            bp = lax.rem(b + 1, nb)
            planes = [halves(src, p, b) for p in range(2)]
            for p in range(2):
                rates = [
                    [vel_ref[d, p, b, :, half(h)].astype(jnp.float32) for d in range(6)]
                    for h in range(2)
                ]
                new = stencil(
                    planes[p],
                    planes[1 - p],
                    1.0 if p == 0 else -1.0,
                    halves(src, p, bm),
                    halves(src, p, bp),
                    rates,
                    masks,
                )
                for h in range(2):
                    base[p, b, :, half(h)] = new[h]

        @pl.loop(0, chunks)
        def _(ch):
            for p in range(2):
                edge = halo_receive(step, p, ch)
                sign = 0.5 if p == 0 else -0.5
                fresh = []
                for h in range(2):
                    row = []
                    for i in range(size):
                        b = ch + chunks * i
                        rate = vel_ref[0, p, b, :, half(h)].astype(jnp.float32)
                        new = base[p, b, :, half(h)] + (0.06 + sign * rate) * edge[h][i]
                        dst[p, b, :, half(h)] = new
                        row.append(new)
                    fresh.append(row)
                if step < STEPS - 1:
                    halo_send(step + 1, 1 - p, ch, fresh)

            if step == STEPS - 1:

                @pl.loop(0, size)
                def _(i):
                    b = ch + chunks * lax.rem(i + md // chunks + size // 2, size)
                    encode_planes(
                        lambda h: dst[0, b, :, half(h)], lambda h: dst[1, b, :, half(h)],
                        b, out_w, out_u,
                    )

                    @pl.when(b != md)
                    def _():
                        for copy in spread(*ph0, md, b):
                            copy.start()

    for p in range(2):
        line[2 * md + p] = last[p, md]

    @pl.loop(0, nd - 1)
    def _(i):
        d = dom_peer(i, -1)
        arrive(*ph0, md, d)
        for h in range(2):
            x, y = decode(in_w[d, :, half(h)], in_u[d, pl.ds(h, 1), :])
            line[2 * d, :, half(h)] = x
            line[2 * d + 1, :, half(h)] = y

    fetch.wait()

    for h in range(2):
        tops = []
        for k in range(HALF):
            for j in (k, k + 8):
                s = slab_of(j)
                g = s & (-s)
                w = jnp.where(s == 0, 0.0, 0.5)
                low, up = (s - g) & (ns - 1), (s + g) & (ns - 1)
                t = line[s, :, half(h)] - w * (line[low, :, half(h)] + line[up, :, half(h)])
                tops.append(t)
        top = functools.reduce(jnp.maximum, [jnp.abs(t) for t in tops])
        e = exponent(jnp.maximum(top, 1e-30))
        inverse = scale(e, -1)
        words = [code(tops[2 * k], tops[2 * k + 1], inverse) for k in range(HALF)]
        block = jnp.stack(words + [e, jnp.zeros_like(e)], axis=0)
        tsend[:, :, half(h)] = jnp.swapaxes(block, 0, 1)

    ph1 = (((tsend, tall),), 1, "comp")
    exchange_start(*ph1, mc, nc)
    tall[mc] = tsend[mc]
    exchange_wait(*ph1, mc, nc)

    blocks = []
    for c in range(nc):
        blocks.extend(decode(tall[c], scale(tall[c, pl.ds(HALF, 1), :], 1)))
    t = jnp.concatenate(blocks, axis=0)
    m = mix[...]
    acc = None
    for part in range(2):
        piece = t.astype(jnp.bfloat16)
        t = t - piece.astype(jnp.float32)
        prod = jnp.dot(m, piece, preferred_element_type=jnp.float32)
        acc = prod if acc is None else acc + prod
    mark = lax.broadcasted_iota(jnp.int32, (8, 256), 0) == HALF
    for c in range(nc):
        x = acc[c * ROWS : c * ROWS + 8]
        y = acc[c * ROWS + 8 : c * ROWS + 16]
        top = fold(jnp.maximum(jnp.abs(x), jnp.abs(y)), 0, jnp.maximum)
        e = exponent(jnp.maximum(top, 1e-30))
        eback[c] = jnp.where(mark, e, code(x, y, scale(e, -1)))

    ph2 = (((eback, erecv),), 2, "comp")
    exchange_start(*ph2, mc, nc)
    erecv[mc] = eback[mc]
    exchange_wait(*ph2, mc, nc)

    for h in range(2):
        words = jnp.swapaxes(erecv[:, :, half(h)], 0, 1)
        unit = scale(words[HALF], 1)
        for k in range(HALF):
            x, y = decode(words[k], unit)
            ez[k, :, half(h)] = x
            ez[k + 8, :, half(h)] = y
    ez[ZERO] = jnp.zeros(ez.shape[1:], jnp.float32)

    n = 2 * nd
    for q in range(4):
        if q % 2 * 8 >= nrow:
            continue
        r = (pl.ds(q % 2 * 8, min(8, nrow)), pl.ds(q // 2 * 128, 128))
        planes = {}
        planes[0] = ez[(slot_of(0), *r)]
        gap = n // 2
        while gap >= 1:
            for s in range(gap, n, 2 * gap):
                planes[s] = ez[(slot_of(s), *r)] + 0.5 * (
                    planes[(s - gap) % n] + planes[(s + gap) % n]
                )
            gap //= 2
        for s in range(n):
            osend[(s, *r)] = planes[s]

    ph3 = (((out2_w, in2_w), (out2_u, in2_u)), 3, "dom")

    @pl.loop(0, nd - 1)
    def _(i):
        d = dom_peer(i, 1)
        encode_planes(
            lambda h: osend[2 * d, :, half(h)],
            lambda h: osend[2 * d + 1, :, half(h)],
            d, out2_w, out2_u,
        )
        for copy in spread(*ph3, md, d):
            copy.start()

    @pl.loop(0, chunks)
    def _(ch):
        for step in range(STEPS):
            for copy in halo(step, 0, ch) + halo(step, 1, ch):
                copy.wait_send()

    def sent(ph, me, k):
        @pl.loop(1, k)
        def _(i):
            for copy in spread(*ph, me, lax.rem(me + i, k)):
                copy.wait_send()

    sent(ph0, md, nd)
    sent(ph1, mc, nc)
    sent(ph2, mc, nc)

    own = coef_ref[mc].astype(jnp.float32)

    for p in range(2):
        out_ref[p, md] = own * last[p, md] + osend[2 * md + p]

    @pl.loop(0, nd - 1)
    def _(i):
        d = dom_peer(i, -1)
        arrive(*ph3, md, d)
        for h in range(2):
            both = decode(in2_w[d, :, half(h)], in2_u[d, pl.ds(h, 1), :])
            for p in range(2):
                out_ref[p, d, :, half(h)] = own * last[p, d, :, half(h)] + both[p]

    sent(ph3, md, nd)


def local(density, velocity, coefficients, owner_lists):
    nc = lax.axis_size("comp")
    nd = lax.axis_size("dom")
    _, planes, nb, nrow, lanes = density.shape
    f32 = jnp.float32
    chunks = min(CHUNKS, nb // 2)
    smem = pl.BlockSpec(memory_space=pltpu.SMEM)
    vmem = pl.BlockSpec(memory_space=pltpu.VMEM)
    out = pl.pallas_call(
        functools.partial(kernel, nc, nd),
        out_shape=jax.ShapeDtypeStruct((planes, nb, nrow, lanes), f32),
        in_specs=[smem, vmem, vmem, vmem],
        out_specs=vmem,
        scratch_shapes=[
            pltpu.VMEM((2, planes, nb, nrow, lanes), f32),
            *[pltpu.VMEM((STEPS, 2, chunks, nb // chunks // 2, nrow, lanes), jnp.int32)] * 2,
            *[pltpu.VMEM((STEPS, 2, chunks, 2, 128), f32)] * 2,
            pltpu.VMEM((planes, nb, nrow, lanes), f32),
            pltpu.VMEM((planes * nd, nrow, lanes), f32),
            *[pltpu.VMEM((nc, 8, lanes), jnp.int32)] * 4,
            pltpu.VMEM((ZERO + 1, nrow, lanes), f32),
            pltpu.VMEM((planes * nd, nrow, lanes), f32),
            *[pltpu.VMEM((nd, nrow, lanes), jnp.int32)] * 4,
            *[pltpu.VMEM((nd, 2, 128), f32)] * 4,
            pltpu.VMEM((nc * ROWS, nc * ROWS), jnp.bfloat16),
            pltpu.VMEM((nc, pl.cdiv(owner_lists.shape[0], 128) * 128), jnp.int32),
            pltpu.VMEM((16, 128), jnp.int32),
            pltpu.VMEM((8, 128), jnp.int32),
            pltpu.SMEM((16, 128), jnp.int32),
            pltpu.SemaphoreType.DMA,
            pltpu.SemaphoreType.DMA((2, STEPS, 2, chunks)),
            pltpu.SemaphoreType.DMA((2, STEPS, 2, chunks)),
            pltpu.SemaphoreType.DMA((4, 2, max(nc, nd))),
            pltpu.SemaphoreType.DMA((4, 2, max(nc, nd))),
        ],
        compiler_params=pltpu.CompilerParams(collective_id=0, has_side_effects=True),
    )(coefficients, owner_lists.T, density[0], velocity[0])
    return out[None]


def solution(mesh):
    in_specs = (
        P("comp", "dom", None, None, None),
        P("comp", None, "dom", None, None, None),
        P(),
        P(),
    )
    out_specs = P("comp", "dom", None, None, None)
    return jax.shard_map(local, mesh=mesh, in_specs=in_specs, out_specs=out_specs, check_vma=False)
```

```python
import functools

import jax
import jax.numpy as jnp
import numpy as np
from jax import lax
from jax.experimental import pallas as pl
from jax.experimental.pallas import tpu as pltpu
from jax.sharding import PartitionSpec as P

STEPS = 4
E_STRIDE, E_EXT = 4, 8
F_STRIDE, F_EXT = 1, 4
ROWS = 16
HALF = 6
ZERO = 16
CHUNKS = 4


def fold(x, axis, op):
    shift = x.shape[axis] // 2
    while shift:
        x = op(x, pltpu.roll(x, shift, axis))
        shift //= 2
    return x


def tables(lists_ref, coef_ref, padded, table, comb, mix, nc, ns):
    i32 = jnp.int32
    depth, blocks = lists_ref.shape
    lane = lax.broadcasted_iota(i32, (8, 128), 1)
    sub = lax.broadcasted_iota(i32, (8, 128), 0)
    tiles = max(1, nc * ns // 128)
    per = 128 // ns
    total = nc * ns

    padded[...] = jnp.full(padded.shape, -1, i32)
    padded[:, pl.ds(0, blocks)] = lists_ref[...]
    slab = lax.broadcasted_iota(i32, (total, 128), 0)
    wide = lax.broadcasted_iota(i32, (total, 128), 1)
    number = jnp.zeros((total, 128), i32)
    for t in range(padded.shape[1] // 128):
        rows = padded[:, pl.ds(t * 128, 128)]
        own = jnp.broadcast_to(rows[:, None, :], (nc, ns, 128)).reshape(total, 128)
        found = (rows[0:1] == slab) | (rows[1:2] == slab) | (own == slab)
        found = found & (rows[1:2] >= 0)
        number = jnp.maximum(number, jnp.where(found, wide + (t * 128 + 1), 0))
    number = fold(number, 1, jnp.maximum)
    number = jnp.where(wide == slab % 128, number, 0)

    ident = jnp.zeros((8, 128), i32)
    for r in range(tiles):
        part = number[r * 128 : min(r * 128 + 128, total)]
        part = jnp.sum(part.reshape(-1, 8, 128), axis=0)
        ident = jnp.where(sub == r, fold(part, 0, jnp.add), ident)
    place = lane % ns
    one = jnp.where(ident > 0, 1, 0)
    count = one
    shift = 1
    while shift < ns:
        count = count + jnp.where(place >= shift, pltpu.roll(count, shift, 1), 0)
        shift *= 2
    slot = count - 1 + jnp.where(count > HALF, 8 - HALF, 0)
    slot = jnp.where(ident > 0, slot, ZERO)
    table[pl.ds(0, 8), :] = slot
    both = jnp.where(ident > 0, ident * 64 + place, 0)
    comb[pl.ds(0, 8), :] = both

    lane2 = lax.broadcasted_iota(i32, (ROWS, 128), 1)
    slot2 = lax.broadcasted_iota(i32, (ROWS, 128), 0)
    columns = []
    for c in range(nc):
        r = c // per
        row = jnp.broadcast_to(table[pl.ds(r, 1), :], (ROWS, 128))
        val = jnp.broadcast_to(comb[pl.ds(r, 1), :], (ROWS, 128))
        mine = (row == slot2) & (lane2 // ns == c % per)
        columns.append(fold(jnp.where(mine, val, 0), 1, jnp.add))

    groups = 128 // ROWS
    width = nc * ROWS
    srow = jnp.zeros((8, 128), i32)
    across = []
    for t in range(0, nc, groups):
        line = jnp.zeros((ROWS, 128), i32)
        for c in range(t, min(t + groups, nc)):
            diag = lane2 == slot2 + (c - t) * ROWS
            line = line + jnp.where(diag, columns[c], 0)
        line = fold(line[:8] + line[8:], 0, jnp.add)
        across.append(jnp.concatenate([line, line], axis=0))
        srow = jnp.where(sub == t // groups, line % 64, srow)
    table[pl.ds(8, 8), :] = srow

    span = min(128, width)
    for t, wide in enumerate(across):
        owner = lane2 // ROWS + t * groups
        weight = jnp.zeros((ROWS, 128), i32)
        for c in range(nc):
            weight = jnp.where(owner == c, coef_ref[c], weight)
        for c in range(nc):
            same = (columns[c] // 64 == wide // 64) & (wide > 0) & (owner != c)
            piece = jnp.where(same, weight, 0).astype(jnp.float32).astype(jnp.bfloat16)
            mix[pl.ds(c * ROWS, ROWS), pl.ds(t * 128, span)] = piece[:, :span]


def peak(values):
    m = functools.reduce(jnp.maximum, [jnp.abs(v) for v in values])
    if m.shape[0] > 8:
        m = jnp.maximum(m[:8], m[8:])
    return jnp.maximum(fold(m, 0, jnp.maximum)[0:1], 1e-30)


def code(a, b, inverse):
    qa = jnp.floor(a * inverse + 0.5).astype(jnp.int32)
    qb = jnp.floor(b * inverse + 0.5).astype(jnp.int32)
    return (qa << 16) | (qb & 0xFFFF)


def decode(word, unit):
    a = (word >> 16).astype(jnp.float32) * unit
    b = ((word << 16) >> 16).astype(jnp.float32) * unit
    return a, b


LEVELS = 32767.0
FINE = 4096.0


def exponent(top):
    return jnp.ceil(jnp.log2(top) * FINE).astype(jnp.int32) + 1


def scale(e, sign):
    power = jnp.exp2(e.astype(jnp.float32) * (sign / FINE))
    return power * (1.0 / 32700.0) if sign > 0 else power * 32700.0


def stencil(cur, beside, sign, left, right, rates, masks):
    e_last, e_first, f_last, f_first, d_low, d_high = masks
    out = []
    down = [pltpu.roll(x, 32, 1) for x in cur]
    up = [pltpu.roll(x, 96, 1) for x in cur]
    for h in range(2):
        x = cur[h]
        pairs = [(right[h], left[h])]
        n = x.shape[0]
        pairs.append((pltpu.roll(x, n - 1, 0), pltpu.roll(x, 1, 0)))
        pairs.append(
            (jnp.where(d_high, up[1 - h], up[h]), jnp.where(d_low, down[1 - h], down[h]))
        )
        pairs.append(
            (
                jnp.where(e_last, pltpu.roll(x, 28, 1), pltpu.roll(x, 124, 1)),
                jnp.where(e_first, pltpu.roll(x, 100, 1), pltpu.roll(x, 4, 1)),
            )
        )
        pairs.append(
            (
                jnp.where(f_last, pltpu.roll(x, 3, 1), pltpu.roll(x, 127, 1)),
                jnp.where(f_first, pltpu.roll(x, 125, 1), pltpu.roll(x, 1, 1)),
            )
        )
        total = None
        drift = None
        for d, (fwd, bwd) in enumerate(pairs):
            s = fwd + bwd
            m = rates[h][d + 1] * (fwd - bwd)
            total = s if total is None else total + s
            drift = m if drift is None else drift + m
        near = (0.06 - sign * 0.5 * rates[h][0]) * beside[h]
        out.append(0.28 * x + near + 0.06 * total - 0.5 * drift)
    return out


def kernel(
    nc, nd,
    coef_ref, lists_ref, dens_ref, vel_ref,
    out_ref,
    ubuf, hs, hr, hs_unit, hr_unit, base, line, tsend, tall, eback, erecv, ez, osend,
    out_w, in_w, out2_w, in2_w, out_u, in_u, out2_u, in2_u, mix, padded, table, comb, tab,
    tab_sem, hs_sem, hr_sem, a_sem, b_sem,
):
    mc = lax.axis_index("comp")
    md = lax.axis_index("dom")
    nb = dens_ref.shape[1]
    chunks = min(CHUNKS, nb // 2)
    size = nb // chunks
    up_d = lax.rem(md + 1, nd)
    dn_d = lax.rem(md + nd - 1, nd)

    barrier = pltpu.get_barrier_semaphore()

    @pl.loop(1, nd)
    def _(i):
        pl.semaphore_signal(barrier, inc=1, device_id={"dom": lax.rem(md + i, nd)})

    @pl.loop(1, nc)
    def _(i):
        pl.semaphore_signal(barrier, inc=1, device_id={"comp": lax.rem(mc + i, nc)})

    def halo(step, way, ch):
        peer = {"dom": up_d if way == 0 else dn_d}
        return [
            pltpu.make_async_remote_copy(
                src_ref=src.at[step, way, ch],
                dst_ref=dst.at[step, way, ch],
                send_sem=hs_sem.at[kind, step, way, ch],
                recv_sem=hr_sem.at[kind, step, way, ch],
                device_id=peer,
            )
            for kind, (src, dst) in enumerate(((hs, hr), (hs_unit, hr_unit)))
        ]

    def half(h):
        return pl.ds(h * 128, 128)

    pair = size // 2

    def halo_code(step, way, ch, values):
        for h in range(2):
            vals = values[h]
            top = peak(vals)
            inverse = LEVELS / top
            for i in range(pair):
                hs[step, way, ch, i, :, half(h)] = code(vals[i], vals[i + pair], inverse)
            hs_unit[step, way, ch, pl.ds(h, 1), :] = top * (1.0 / LEVELS)

    def halo_start(step, way, ch):
        for copy in halo(step, way, ch):
            copy.start()

    def halo_receive(step, way, ch):
        for copy in halo(step, way, ch):
            copy.wait_recv()
        out = []
        for h in range(2):
            unit = hr_unit[step, way, ch, pl.ds(h, 1), :]
            both = [decode(hr[step, way, ch, i, :, half(h)], unit) for i in range(pair)]
            out.append([x for x, _ in both] + [y for _, y in both])
        return out

    @pl.loop(0, chunks)
    def _(ch):
        for way in range(2):
            halo_code(
                0, way, ch,
                [
                    [dens_ref[1 - way, ch + chunks * i, :, half(h)] for i in range(size)]
                    for h in range(2)
                ],
            )

    ns = 2 * nd
    tables(lists_ref, coef_ref, padded, table, comb, mix, nc, ns)
    fetch = pltpu.make_async_copy(table, tab, tab_sem)
    fetch.start()

    pl.semaphore_wait(barrier, nd + nc - 2)

    @pl.loop(0, chunks)
    def _(ch):
        for way in range(2):
            halo_start(0, way, ch)

    per = 128 // ns

    def slot_of(s):
        return tab[mc // per, (mc % per) * ns + s]

    def slab_of(j):
        at = mc * ROWS + j
        return tab[8 + at // 128, at % 128]

    nrow = dens_ref.shape[2]
    lane = lax.broadcasted_iota(jnp.int32, (nrow, 128), 1)
    e_idx = (lane // E_STRIDE) % E_EXT
    f_idx = lane % F_EXT
    masks = (
        e_idx == E_EXT - 1, e_idx == 0, f_idx == F_EXT - 1, f_idx == 0,
        lane < 32, lane >= 96,
    )

    def halves(ref, *idx):
        return [ref[(*idx, slice(None), pl.ds(h * 128, 128))].astype(jnp.float32) for h in range(2)]

    last = ubuf.at[(STEPS - 1) % 2]

    def spread(refs, phase, axis, me, peer):
        return [
            pltpu.make_async_remote_copy(
                src_ref=src.at[peer],
                dst_ref=dst.at[me],
                send_sem=a_sem.at[phase, kind, peer],
                recv_sem=b_sem.at[phase, kind, me],
                device_id={axis: peer},
            )
            for kind, (src, dst) in enumerate(refs)
        ]

    def arrive(refs, phase, axis, me, peer):
        for kind, (src, dst) in enumerate(refs):
            pltpu.make_async_remote_copy(
                src_ref=src.at[peer],
                dst_ref=dst.at[peer],
                send_sem=a_sem.at[phase, kind, peer],
                recv_sem=b_sem.at[phase, kind, peer],
                device_id={axis: peer},
            ).wait_recv()

    nz, nx = nd // 2, nc // 4

    def swing(k, n):
        return n // 2 + k // 2 - (k % 2) * k

    def dom_peer(i, sign):
        z = lax.rem(md % nz + sign * swing(lax.rem(i, nz), nz) + nz, nz)
        y = lax.rem(md // nz + 1 - i // nz, 2)
        return y * nz + z

    def comp_peer(i, sign):
        q = i // 2
        x = lax.rem(mc // 4 + sign * swing(q % nx, nx) + nx, nx)
        y = lax.rem((mc // 2) % 2 + 1 - q // nx, 2)
        core = lax.rem(mc % 2 + 1 - i % 2, 2)
        return (x * 2 + y) * 2 + core

    def exchange_start(refs, phase, axis, me, n):
        @pl.loop(0, n - 1)
        def _(i):
            for copy in spread(refs, phase, axis, me, comp_peer(i, 1)):
                copy.start()

    def exchange_wait(refs, phase, axis, me, n):
        @pl.loop(0, n - 1)
        def _(i):
            arrive(refs, phase, axis, me, comp_peer(i, -1))

    def encode_planes(first, second, d, words, units):
        for h in range(2):
            x, y = first(h), second(h)
            top = peak([x, y])
            words[d, :, half(h)] = code(x, y, LEVELS / top)
            units[d, pl.ds(h, 1), :] = top * (1.0 / LEVELS)

    ph0 = (((out_w, in_w), (out_u, in_u)), 0, "dom")

    for step in range(STEPS):
        src = dens_ref if step == 0 else ubuf.at[(step - 1) % 2]
        dst = ubuf.at[step % 2]

        @pl.loop(0, nb)
        def _(b):
            bm = lax.rem(b + nb - 1, nb)
            bp = lax.rem(b + 1, nb)
            planes = [halves(src, p, b) for p in range(2)]
            for p in range(2):
                rates = [
                    [vel_ref[d, p, b, :, half(h)].astype(jnp.float32) for d in range(6)]
                    for h in range(2)
                ]
                new = stencil(
                    planes[p],
                    planes[1 - p],
                    1.0 if p == 0 else -1.0,
                    halves(src, p, bm),
                    halves(src, p, bp),
                    rates,
                    masks,
                )
                for h in range(2):
                    base[p, b, :, half(h)] = new[h]

        @pl.loop(0, chunks)
        def _(ch):
            for p in range(2):
                edge = halo_receive(step, p, ch)
                sign = 0.5 if p == 0 else -0.5
                fresh = []
                for h in range(2):
                    row = []
                    for i in range(size):
                        b = ch + chunks * i
                        rate = vel_ref[0, p, b, :, half(h)].astype(jnp.float32)
                        new = base[p, b, :, half(h)] + (0.06 + sign * rate) * edge[h][i]
                        dst[p, b, :, half(h)] = new
                        row.append(new)
                    fresh.append(row)
                if step < STEPS - 1:
                    halo_code(step + 1, 1 - p, ch, fresh)
                    halo_start(step + 1, 1 - p, ch)

            if step == STEPS - 1:

                @pl.loop(0, size)
                def _(i):
                    b = ch + chunks * lax.rem(i + md // chunks + size // 2, size)
                    encode_planes(
                        lambda h: dst[0, b, :, half(h)], lambda h: dst[1, b, :, half(h)],
                        b, out_w, out_u,
                    )

                    @pl.when(b != md)
                    def _():
                        for copy in spread(*ph0, md, b):
                            copy.start()

    for p in range(2):
        line[2 * md + p] = last[p, md]

    @pl.loop(0, nd - 1)
    def _(i):
        d = dom_peer(i, -1)
        arrive(*ph0, md, d)
        for h in range(2):
            x, y = decode(in_w[d, :, half(h)], in_u[d, pl.ds(h, 1), :])
            line[2 * d, :, half(h)] = x
            line[2 * d + 1, :, half(h)] = y

    fetch.wait()

    for h in range(2):
        tops = []
        for k in range(HALF):
            for j in (k, k + 8):
                s = slab_of(j)
                g = s & (-s)
                w = jnp.where(s == 0, 0.0, 0.5)
                low, up = (s - g) & (ns - 1), (s + g) & (ns - 1)
                t = line[s, :, half(h)] - w * (line[low, :, half(h)] + line[up, :, half(h)])
                tops.append(t)
        top = functools.reduce(jnp.maximum, [jnp.abs(t) for t in tops])
        e = exponent(jnp.maximum(top, 1e-30))
        inverse = scale(e, -1)
        words = [code(tops[2 * k], tops[2 * k + 1], inverse) for k in range(HALF)]
        block = jnp.stack(words + [e, jnp.zeros_like(e)], axis=0)
        tsend[:, :, half(h)] = jnp.swapaxes(block, 0, 1)

    ph1 = (((tsend, tall),), 1, "comp")
    exchange_start(*ph1, mc, nc)
    tall[mc] = tsend[mc]
    exchange_wait(*ph1, mc, nc)

    blocks = []
    for c in range(nc):
        blocks.extend(decode(tall[c], scale(tall[c, pl.ds(HALF, 1), :], 1)))
    t = jnp.concatenate(blocks, axis=0)
    m = mix[...]
    acc = None
    for part in range(2):
        piece = t.astype(jnp.bfloat16)
        t = t - piece.astype(jnp.float32)
        prod = jnp.dot(m, piece, preferred_element_type=jnp.float32)
        acc = prod if acc is None else acc + prod
    mark = lax.broadcasted_iota(jnp.int32, (8, 256), 0) == HALF
    for c in range(nc):
        x = acc[c * ROWS : c * ROWS + 8]
        y = acc[c * ROWS + 8 : c * ROWS + 16]
        top = fold(jnp.maximum(jnp.abs(x), jnp.abs(y)), 0, jnp.maximum)
        e = exponent(jnp.maximum(top, 1e-30))
        eback[c] = jnp.where(mark, e, code(x, y, scale(e, -1)))

    ph2 = (((eback, erecv),), 2, "comp")
    exchange_start(*ph2, mc, nc)
    erecv[mc] = eback[mc]
    exchange_wait(*ph2, mc, nc)

    for h in range(2):
        words = jnp.swapaxes(erecv[:, :, half(h)], 0, 1)
        unit = scale(words[HALF], 1)
        for k in range(HALF):
            x, y = decode(words[k], unit)
            ez[k, :, half(h)] = x
            ez[k + 8, :, half(h)] = y
    ez[ZERO] = jnp.zeros(ez.shape[1:], jnp.float32)

    n = 2 * nd
    for q in range(4):
        if q % 2 * 8 >= nrow:
            continue
        r = (pl.ds(q % 2 * 8, min(8, nrow)), pl.ds(q // 2 * 128, 128))
        planes = {}
        planes[0] = ez[(slot_of(0), *r)]
        gap = n // 2
        while gap >= 1:
            for s in range(gap, n, 2 * gap):
                planes[s] = ez[(slot_of(s), *r)] + 0.5 * (
                    planes[(s - gap) % n] + planes[(s + gap) % n]
                )
            gap //= 2
        for s in range(n):
            osend[(s, *r)] = planes[s]

    ph3 = (((out2_w, in2_w), (out2_u, in2_u)), 3, "dom")

    @pl.loop(0, nd - 1)
    def _(i):
        d = dom_peer(i, 1)
        encode_planes(
            lambda h: osend[2 * d, :, half(h)],
            lambda h: osend[2 * d + 1, :, half(h)],
            d, out2_w, out2_u,
        )
        for copy in spread(*ph3, md, d):
            copy.start()

    @pl.loop(0, chunks)
    def _(ch):
        for step in range(STEPS):
            for copy in halo(step, 0, ch) + halo(step, 1, ch):
                copy.wait_send()

    def sent(ph, me, k):
        @pl.loop(1, k)
        def _(i):
            for copy in spread(*ph, me, lax.rem(me + i, k)):
                copy.wait_send()

    sent(ph0, md, nd)
    sent(ph1, mc, nc)
    sent(ph2, mc, nc)

    own = coef_ref[mc].astype(jnp.float32)

    for p in range(2):
        out_ref[p, md] = own * last[p, md] + osend[2 * md + p]

    @pl.loop(0, nd - 1)
    def _(i):
        d = dom_peer(i, -1)
        arrive(*ph3, md, d)
        for h in range(2):
            both = decode(in2_w[d, :, half(h)], in2_u[d, pl.ds(h, 1), :])
            for p in range(2):
                out_ref[p, d, :, half(h)] = own * last[p, d, :, half(h)] + both[p]

    sent(ph3, md, nd)


def local(density, velocity, coefficients, owner_lists):
    nc = lax.axis_size("comp")
    nd = lax.axis_size("dom")
    _, planes, nb, nrow, lanes = density.shape
    f32 = jnp.float32
    chunks = min(CHUNKS, nb // 2)
    smem = pl.BlockSpec(memory_space=pltpu.SMEM)
    vmem = pl.BlockSpec(memory_space=pltpu.VMEM)
    out = pl.pallas_call(
        functools.partial(kernel, nc, nd),
        out_shape=jax.ShapeDtypeStruct((planes, nb, nrow, lanes), f32),
        in_specs=[smem, vmem, vmem, vmem],
        out_specs=vmem,
        scratch_shapes=[
            pltpu.VMEM((2, planes, nb, nrow, lanes), f32),
            *[pltpu.VMEM((STEPS, 2, chunks, nb // chunks // 2, nrow, lanes), jnp.int32)] * 2,
            *[pltpu.VMEM((STEPS, 2, chunks, 2, 128), f32)] * 2,
            pltpu.VMEM((planes, nb, nrow, lanes), f32),
            pltpu.VMEM((planes * nd, nrow, lanes), f32),
            *[pltpu.VMEM((nc, 8, lanes), jnp.int32)] * 4,
            pltpu.VMEM((ZERO + 1, nrow, lanes), f32),
            pltpu.VMEM((planes * nd, nrow, lanes), f32),
            *[pltpu.VMEM((nd, nrow, lanes), jnp.int32)] * 4,
            *[pltpu.VMEM((nd, 2, 128), f32)] * 4,
            pltpu.VMEM((nc * ROWS, nc * ROWS), jnp.bfloat16),
            pltpu.VMEM((nc, pl.cdiv(owner_lists.shape[0], 128) * 128), jnp.int32),
            pltpu.VMEM((16, 128), jnp.int32),
            pltpu.VMEM((8, 128), jnp.int32),
            pltpu.SMEM((16, 128), jnp.int32),
            pltpu.SemaphoreType.DMA,
            pltpu.SemaphoreType.DMA((2, STEPS, 2, chunks)),
            pltpu.SemaphoreType.DMA((2, STEPS, 2, chunks)),
            pltpu.SemaphoreType.DMA((4, 2, max(nc, nd))),
            pltpu.SemaphoreType.DMA((4, 2, max(nc, nd))),
        ],
        compiler_params=pltpu.CompilerParams(collective_id=0, has_side_effects=True),
    )(coefficients, owner_lists.T, density[0], velocity[0])
    return out[None]


def solution(mesh):
    in_specs = (
        P("comp", "dom", None, None, None),
        P("comp", None, "dom", None, None, None),
        P(),
        P(),
    )
    out_specs = P("comp", "dom", None, None, None)
    return jax.shard_map(local, mesh=mesh, in_specs=in_specs, out_specs=out_specs, check_vma=False)
```

```python
import functools

import jax
import jax.numpy as jnp
import numpy as np
from jax import lax
from jax.experimental import pallas as pl
from jax.experimental.pallas import tpu as pltpu
from jax.sharding import PartitionSpec as P

STEPS = 4
E_STRIDE, E_EXT = 4, 8
F_STRIDE, F_EXT = 1, 4
ROWS = 16
HALF = 6
ZERO = 16
CHUNKS = 4


def fold(x, axis, op):
    shift = x.shape[axis] // 2
    while shift:
        x = op(x, pltpu.roll(x, shift, axis))
        shift //= 2
    return x


def tables(lists_ref, coef_ref, padded, table, comb, mix, nc, ns):
    i32 = jnp.int32
    depth, blocks = lists_ref.shape
    lane = lax.broadcasted_iota(i32, (8, 128), 1)
    sub = lax.broadcasted_iota(i32, (8, 128), 0)
    tiles = max(1, nc * ns // 128)
    per = 128 // ns
    total = nc * ns

    padded[...] = jnp.full(padded.shape, -1, i32)
    padded[:, pl.ds(0, blocks)] = lists_ref[...]
    slab = lax.broadcasted_iota(i32, (total, 128), 0)
    wide = lax.broadcasted_iota(i32, (total, 128), 1)
    number = jnp.zeros((total, 128), i32)
    for t in range(padded.shape[1] // 128):
        rows = padded[:, pl.ds(t * 128, 128)]
        own = jnp.broadcast_to(rows[:, None, :], (nc, ns, 128)).reshape(total, 128)
        found = (rows[0:1] == slab) | (rows[1:2] == slab) | (own == slab)
        found = found & (rows[1:2] >= 0)
        number = jnp.maximum(number, jnp.where(found, wide + (t * 128 + 1), 0))
    number = fold(number, 1, jnp.maximum)
    number = jnp.where(wide == slab % 128, number, 0)

    ident = jnp.zeros((8, 128), i32)
    for r in range(tiles):
        part = number[r * 128 : min(r * 128 + 128, total)]
        part = jnp.sum(part.reshape(-1, 8, 128), axis=0)
        ident = jnp.where(sub == r, fold(part, 0, jnp.add), ident)
    place = lane % ns
    one = jnp.where(ident > 0, 1, 0)
    count = one
    shift = 1
    while shift < ns:
        count = count + jnp.where(place >= shift, pltpu.roll(count, shift, 1), 0)
        shift *= 2
    slot = count - 1 + jnp.where(count > HALF, 8 - HALF, 0)
    slot = jnp.where(ident > 0, slot, ZERO)
    table[pl.ds(0, 8), :] = slot
    both = jnp.where(ident > 0, ident * 64 + place, 0)
    comb[pl.ds(0, 8), :] = both

    lane2 = lax.broadcasted_iota(i32, (ROWS, 128), 1)
    slot2 = lax.broadcasted_iota(i32, (ROWS, 128), 0)
    columns = []
    for c in range(nc):
        r = c // per
        row = jnp.broadcast_to(table[pl.ds(r, 1), :], (ROWS, 128))
        val = jnp.broadcast_to(comb[pl.ds(r, 1), :], (ROWS, 128))
        mine = (row == slot2) & (lane2 // ns == c % per)
        columns.append(fold(jnp.where(mine, val, 0), 1, jnp.add))

    groups = 128 // ROWS
    width = nc * ROWS
    srow = jnp.zeros((8, 128), i32)
    across = []
    for t in range(0, nc, groups):
        line = jnp.zeros((ROWS, 128), i32)
        for c in range(t, min(t + groups, nc)):
            diag = lane2 == slot2 + (c - t) * ROWS
            line = line + jnp.where(diag, columns[c], 0)
        line = fold(line[:8] + line[8:], 0, jnp.add)
        across.append(jnp.concatenate([line, line], axis=0))
        srow = jnp.where(sub == t // groups, line % 64, srow)
    table[pl.ds(8, 8), :] = srow

    span = min(128, width)
    for t, wide in enumerate(across):
        owner = lane2 // ROWS + t * groups
        weight = jnp.zeros((ROWS, 128), i32)
        for c in range(nc):
            weight = jnp.where(owner == c, coef_ref[c], weight)
        for c in range(nc):
            same = (columns[c] // 64 == wide // 64) & (wide > 0) & (owner != c)
            piece = jnp.where(same, weight, 0).astype(jnp.float32).astype(jnp.bfloat16)
            mix[pl.ds(c * ROWS, ROWS), pl.ds(t * 128, span)] = piece[:, :span]


def peak(values):
    m = functools.reduce(jnp.maximum, [jnp.abs(v) for v in values])
    if m.shape[0] > 8:
        m = jnp.maximum(m[:8], m[8:])
    return jnp.maximum(fold(m, 0, jnp.maximum)[0:1], 1e-30)


def code(a, b, inverse):
    qa = jnp.floor(a * inverse + 0.5).astype(jnp.int32)
    qb = jnp.floor(b * inverse + 0.5).astype(jnp.int32)
    return (qa << 16) | (qb & 0xFFFF)


def decode(word, unit):
    a = (word >> 16).astype(jnp.float32) * unit
    b = ((word << 16) >> 16).astype(jnp.float32) * unit
    return a, b


LEVELS = 32767.0
FINE = 4096.0


def exponent(top):
    return jnp.ceil(jnp.log2(top) * FINE).astype(jnp.int32) + 1


def scale(e, sign):
    power = jnp.exp2(e.astype(jnp.float32) * (sign / FINE))
    return power * (1.0 / 32700.0) if sign > 0 else power * 32700.0


def stencil(cur, beside, sign, left, right, rates, masks):
    e_last, e_first, f_last, f_first, d_low, d_high = masks
    out = []
    down = [pltpu.roll(x, 32, 1) for x in cur]
    up = [pltpu.roll(x, 96, 1) for x in cur]
    for h in range(2):
        x = cur[h]
        pairs = [(right[h], left[h])]
        n = x.shape[0]
        pairs.append((pltpu.roll(x, n - 1, 0), pltpu.roll(x, 1, 0)))
        pairs.append(
            (jnp.where(d_high, up[1 - h], up[h]), jnp.where(d_low, down[1 - h], down[h]))
        )
        pairs.append(
            (
                jnp.where(e_last, pltpu.roll(x, 28, 1), pltpu.roll(x, 124, 1)),
                jnp.where(e_first, pltpu.roll(x, 100, 1), pltpu.roll(x, 4, 1)),
            )
        )
        pairs.append(
            (
                jnp.where(f_last, pltpu.roll(x, 3, 1), pltpu.roll(x, 127, 1)),
                jnp.where(f_first, pltpu.roll(x, 125, 1), pltpu.roll(x, 1, 1)),
            )
        )
        total = None
        drift = None
        for d, (fwd, bwd) in enumerate(pairs):
            s = fwd + bwd
            m = rates[h][d + 1] * (fwd - bwd)
            total = s if total is None else total + s
            drift = m if drift is None else drift + m
        near = (0.06 - sign * 0.5 * rates[h][0]) * beside[h]
        out.append(0.28 * x + near + 0.06 * total - 0.5 * drift)
    return out


def kernel(
    nc, nd,
    coef_ref, lists_ref, dens_ref, vel_ref,
    out_ref,
    ubuf, hs, hr, hs_unit, hr_unit, base, line, tsend, tall, eback, erecv, ez, osend,
    out_w, in_w, out2_w, in2_w, out_u, in_u, out2_u, in2_u, mix, padded, table, comb, tab,
    tab_sem, hs_sem, hr_sem, a_sem, b_sem,
):
    mc = lax.axis_index("comp")
    md = lax.axis_index("dom")
    nb = dens_ref.shape[1]
    chunks = min(CHUNKS, nb // 2)
    size = nb // chunks
    up_d = lax.rem(md + 1, nd)
    dn_d = lax.rem(md + nd - 1, nd)

    barrier = pltpu.get_barrier_semaphore()

    @pl.loop(1, nd)
    def _(i):
        pl.semaphore_signal(barrier, inc=1, device_id={"dom": lax.rem(md + i, nd)})

    @pl.loop(1, nc)
    def _(i):
        pl.semaphore_signal(barrier, inc=1, device_id={"comp": lax.rem(mc + i, nc)})

    def halo(step, way, ch):
        peer = {"dom": up_d if way == 0 else dn_d}
        return [
            pltpu.make_async_remote_copy(
                src_ref=src.at[step, way, ch],
                dst_ref=dst.at[step, way, ch],
                send_sem=hs_sem.at[kind, step, way, ch],
                recv_sem=hr_sem.at[kind, step, way, ch],
                device_id=peer,
            )
            for kind, (src, dst) in enumerate(((hs, hr), (hs_unit, hr_unit)))
        ]

    def half(h):
        return pl.ds(h * 128, 128)

    pair = size // 2

    def halo_code(step, way, ch, values):
        for h in range(2):
            vals = values[h]
            top = peak(vals)
            inverse = LEVELS / top
            for i in range(pair):
                hs[step, way, ch, i, :, half(h)] = code(vals[i], vals[i + pair], inverse)
            hs_unit[step, way, ch, pl.ds(h, 1), :] = top * (1.0 / LEVELS)

    def halo_start(step, way, ch):
        for copy in halo(step, way, ch):
            copy.start()

    def halo_receive(step, way, ch):
        for copy in halo(step, way, ch):
            copy.wait_recv()
        out = []
        for h in range(2):
            unit = hr_unit[step, way, ch, pl.ds(h, 1), :]
            both = [decode(hr[step, way, ch, i, :, half(h)], unit) for i in range(pair)]
            out.append([x for x, _ in both] + [y for _, y in both])
        return out

    @pl.loop(0, chunks)
    def _(ch):
        for way in range(2):
            halo_code(
                0, way, ch,
                [
                    [dens_ref[1 - way, ch + chunks * i, :, half(h)] for i in range(size)]
                    for h in range(2)
                ],
            )

    ns = 2 * nd
    tables(lists_ref, coef_ref, padded, table, comb, mix, nc, ns)
    fetch = pltpu.make_async_copy(table, tab, tab_sem)
    fetch.start()

    pl.semaphore_wait(barrier, nd + nc - 2)

    @pl.loop(0, chunks)
    def _(ch):
        for way in range(2):
            halo_start(0, way, ch)

    per = 128 // ns

    def slot_of(s):
        return tab[mc // per, (mc % per) * ns + s]

    def slab_of(j):
        at = mc * ROWS + j
        return tab[8 + at // 128, at % 128]

    nrow = dens_ref.shape[2]
    lane = lax.broadcasted_iota(jnp.int32, (nrow, 128), 1)
    e_idx = (lane // E_STRIDE) % E_EXT
    f_idx = lane % F_EXT
    masks = (
        e_idx == E_EXT - 1, e_idx == 0, f_idx == F_EXT - 1, f_idx == 0,
        lane < 32, lane >= 96,
    )

    def halves(ref, *idx):
        return [ref[(*idx, slice(None), pl.ds(h * 128, 128))].astype(jnp.float32) for h in range(2)]

    last = ubuf.at[(STEPS - 1) % 2]

    def spread(refs, phase, axis, me, peer):
        return [
            pltpu.make_async_remote_copy(
                src_ref=src.at[peer],
                dst_ref=dst.at[me],
                send_sem=a_sem.at[phase, kind, peer],
                recv_sem=b_sem.at[phase, kind, me],
                device_id={axis: peer},
            )
            for kind, (src, dst) in enumerate(refs)
        ]

    def arrive(refs, phase, axis, me, peer):
        for kind, (src, dst) in enumerate(refs):
            pltpu.make_async_remote_copy(
                src_ref=src.at[peer],
                dst_ref=dst.at[peer],
                send_sem=a_sem.at[phase, kind, peer],
                recv_sem=b_sem.at[phase, kind, peer],
                device_id={axis: peer},
            ).wait_recv()

    nz, nx = nd // 2, nc // 4

    def swing(k, n):
        return n // 2 + k // 2 - (k % 2) * k

    def dom_peer(i, sign):
        z = lax.rem(md % nz + sign * swing(lax.rem(i, nz), nz) + nz, nz)
        y = lax.rem(md // nz + 1 - i // nz, 2)
        return y * nz + z

    def comp_peer(i, sign):
        q = i // 2
        x = lax.rem(mc // 4 + sign * swing(q % nx, nx) + nx, nx)
        y = lax.rem((mc // 2) % 2 + 1 - q // nx, 2)
        core = lax.rem(mc % 2 + 1 - i % 2, 2)
        return (x * 2 + y) * 2 + core

    def exchange_start(refs, phase, axis, me, n):
        @pl.loop(0, n - 1, unroll=True)
        def _(i):
            for copy in spread(refs, phase, axis, me, comp_peer(i, 1)):
                copy.start()

    def exchange_wait(refs, phase, axis, me, n):
        @pl.loop(0, n - 1, unroll=True)
        def _(i):
            arrive(refs, phase, axis, me, comp_peer(i, -1))

    def encode_planes(first, second, d, words, units):
        for h in range(2):
            x, y = first(h), second(h)
            top = peak([x, y])
            words[d, :, half(h)] = code(x, y, LEVELS / top)
            units[d, pl.ds(h, 1), :] = top * (1.0 / LEVELS)

    ph0 = (((out_w, in_w), (out_u, in_u)), 0, "dom")

    for step in range(STEPS):
        src = dens_ref if step == 0 else ubuf.at[(step - 1) % 2]
        dst = ubuf.at[step % 2]

        @pl.loop(0, nb)
        def _(b):
            bm = lax.rem(b + nb - 1, nb)
            bp = lax.rem(b + 1, nb)
            planes = [halves(src, p, b) for p in range(2)]
            for p in range(2):
                rates = [
                    [vel_ref[d, p, b, :, half(h)].astype(jnp.float32) for d in range(6)]
                    for h in range(2)
                ]
                new = stencil(
                    planes[p],
                    planes[1 - p],
                    1.0 if p == 0 else -1.0,
                    halves(src, p, bm),
                    halves(src, p, bp),
                    rates,
                    masks,
                )
                for h in range(2):
                    base[p, b, :, half(h)] = new[h]

        @pl.loop(0, chunks)
        def _(ch):
            for p in range(2):
                edge = halo_receive(step, p, ch)
                sign = 0.5 if p == 0 else -0.5
                fresh = []
                for h in range(2):
                    row = []
                    for i in range(size):
                        b = ch + chunks * i
                        rate = vel_ref[0, p, b, :, half(h)].astype(jnp.float32)
                        new = base[p, b, :, half(h)] + (0.06 + sign * rate) * edge[h][i]
                        dst[p, b, :, half(h)] = new
                        row.append(new)
                    fresh.append(row)
                if step < STEPS - 1:
                    halo_code(step + 1, 1 - p, ch, fresh)
                    halo_start(step + 1, 1 - p, ch)

            if step == STEPS - 1:

                @pl.loop(0, size)
                def _(i):
                    b = ch + chunks * lax.rem(i + md // chunks + size // 2, size)
                    encode_planes(
                        lambda h: dst[0, b, :, half(h)], lambda h: dst[1, b, :, half(h)],
                        b, out_w, out_u,
                    )

                    @pl.when(b != md)
                    def _():
                        for copy in spread(*ph0, md, b):
                            copy.start()

    for p in range(2):
        line[2 * md + p] = last[p, md]

    @pl.loop(0, nd - 1, unroll=True)
    def _(i):
        d = dom_peer(i, -1)
        arrive(*ph0, md, d)
        for h in range(2):
            x, y = decode(in_w[d, :, half(h)], in_u[d, pl.ds(h, 1), :])
            line[2 * d, :, half(h)] = x
            line[2 * d + 1, :, half(h)] = y

    fetch.wait()

    for h in range(2):
        tops = []
        for k in range(HALF):
            for j in (k, k + 8):
                s = slab_of(j)
                g = s & (-s)
                w = jnp.where(s == 0, 0.0, 0.5)
                low, up = (s - g) & (ns - 1), (s + g) & (ns - 1)
                t = line[s, :, half(h)] - w * (line[low, :, half(h)] + line[up, :, half(h)])
                tops.append(t)
        top = functools.reduce(jnp.maximum, [jnp.abs(t) for t in tops])
        e = exponent(jnp.maximum(top, 1e-30))
        inverse = scale(e, -1)
        words = [code(tops[2 * k], tops[2 * k + 1], inverse) for k in range(HALF)]
        block = jnp.stack(words + [e, jnp.zeros_like(e)], axis=0)
        tsend[:, :, half(h)] = jnp.swapaxes(block, 0, 1)

    ph1 = (((tsend, tall),), 1, "comp")
    exchange_start(*ph1, mc, nc)
    tall[mc] = tsend[mc]
    exchange_wait(*ph1, mc, nc)

    blocks = []
    for c in range(nc):
        blocks.extend(decode(tall[c], scale(tall[c, pl.ds(HALF, 1), :], 1)))
    t = jnp.concatenate(blocks, axis=0)
    m = mix[...]
    acc = None
    for part in range(2):
        piece = t.astype(jnp.bfloat16)
        t = t - piece.astype(jnp.float32)
        prod = jnp.dot(m, piece, preferred_element_type=jnp.float32)
        acc = prod if acc is None else acc + prod
    mark = lax.broadcasted_iota(jnp.int32, (8, 256), 0) == HALF
    for c in range(nc):
        x = acc[c * ROWS : c * ROWS + 8]
        y = acc[c * ROWS + 8 : c * ROWS + 16]
        top = fold(jnp.maximum(jnp.abs(x), jnp.abs(y)), 0, jnp.maximum)
        e = exponent(jnp.maximum(top, 1e-30))
        eback[c] = jnp.where(mark, e, code(x, y, scale(e, -1)))

    ph2 = (((eback, erecv),), 2, "comp")
    exchange_start(*ph2, mc, nc)
    erecv[mc] = eback[mc]
    exchange_wait(*ph2, mc, nc)

    for h in range(2):
        words = jnp.swapaxes(erecv[:, :, half(h)], 0, 1)
        unit = scale(words[HALF], 1)
        for k in range(HALF):
            x, y = decode(words[k], unit)
            ez[k, :, half(h)] = x
            ez[k + 8, :, half(h)] = y
    ez[ZERO] = jnp.zeros(ez.shape[1:], jnp.float32)

    n = 2 * nd
    for q in range(4):
        if q % 2 * 8 >= nrow:
            continue
        r = (pl.ds(q % 2 * 8, min(8, nrow)), pl.ds(q // 2 * 128, 128))
        planes = {}
        planes[0] = ez[(slot_of(0), *r)]
        gap = n // 2
        while gap >= 1:
            for s in range(gap, n, 2 * gap):
                planes[s] = ez[(slot_of(s), *r)] + 0.5 * (
                    planes[(s - gap) % n] + planes[(s + gap) % n]
                )
            gap //= 2
        for s in range(n):
            osend[(s, *r)] = planes[s]

    ph3 = (((out2_w, in2_w), (out2_u, in2_u)), 3, "dom")

    @pl.loop(0, nd - 1, unroll=True)
    def _(i):
        d = dom_peer(i, 1)
        encode_planes(
            lambda h: osend[2 * d, :, half(h)],
            lambda h: osend[2 * d + 1, :, half(h)],
            d, out2_w, out2_u,
        )
        for copy in spread(*ph3, md, d):
            copy.start()

    @pl.loop(0, chunks)
    def _(ch):
        for step in range(STEPS):
            for copy in halo(step, 0, ch) + halo(step, 1, ch):
                copy.wait_send()

    def sent(ph, me, k):
        @pl.loop(1, k)
        def _(i):
            for copy in spread(*ph, me, lax.rem(me + i, k)):
                copy.wait_send()

    sent(ph0, md, nd)
    sent(ph1, mc, nc)
    sent(ph2, mc, nc)

    own = coef_ref[mc].astype(jnp.float32)

    for p in range(2):
        out_ref[p, md] = own * last[p, md] + osend[2 * md + p]

    @pl.loop(0, nd - 1, unroll=True)
    def _(i):
        d = dom_peer(i, -1)
        for copy in spread(*ph3, md, dom_peer(i, 1)):
            copy.wait_send()
        arrive(*ph3, md, d)
        for h in range(2):
            both = decode(in2_w[d, :, half(h)], in2_u[d, pl.ds(h, 1), :])
            for p in range(2):
                out_ref[p, d, :, half(h)] = own * last[p, d, :, half(h)] + both[p]


def local(density, velocity, coefficients, owner_lists):
    nc = lax.axis_size("comp")
    nd = lax.axis_size("dom")
    _, planes, nb, nrow, lanes = density.shape
    f32 = jnp.float32
    chunks = min(CHUNKS, nb // 2)
    smem = pl.BlockSpec(memory_space=pltpu.SMEM)
    vmem = pl.BlockSpec(memory_space=pltpu.VMEM)
    out = pl.pallas_call(
        functools.partial(kernel, nc, nd),
        out_shape=jax.ShapeDtypeStruct((planes, nb, nrow, lanes), f32),
        in_specs=[smem, vmem, vmem, vmem],
        out_specs=vmem,
        scratch_shapes=[
            pltpu.VMEM((2, planes, nb, nrow, lanes), f32),
            *[pltpu.VMEM((STEPS, 2, chunks, nb // chunks // 2, nrow, lanes), jnp.int32)] * 2,
            *[pltpu.VMEM((STEPS, 2, chunks, 2, 128), f32)] * 2,
            pltpu.VMEM((planes, nb, nrow, lanes), f32),
            pltpu.VMEM((planes * nd, nrow, lanes), f32),
            *[pltpu.VMEM((nc, 8, lanes), jnp.int32)] * 4,
            pltpu.VMEM((ZERO + 1, nrow, lanes), f32),
            pltpu.VMEM((planes * nd, nrow, lanes), f32),
            *[pltpu.VMEM((nd, nrow, lanes), jnp.int32)] * 4,
            *[pltpu.VMEM((nd, 2, 128), f32)] * 4,
            pltpu.VMEM((nc * ROWS, nc * ROWS), jnp.bfloat16),
            pltpu.VMEM((nc, pl.cdiv(owner_lists.shape[0], 128) * 128), jnp.int32),
            pltpu.VMEM((16, 128), jnp.int32),
            pltpu.VMEM((8, 128), jnp.int32),
            pltpu.SMEM((16, 128), jnp.int32),
            pltpu.SemaphoreType.DMA,
            pltpu.SemaphoreType.DMA((2, STEPS, 2, chunks)),
            pltpu.SemaphoreType.DMA((2, STEPS, 2, chunks)),
            pltpu.SemaphoreType.DMA((4, 2, max(nc, nd))),
            pltpu.SemaphoreType.DMA((4, 2, max(nc, nd))),
        ],
        compiler_params=pltpu.CompilerParams(collective_id=0, has_side_effects=True),
    )(coefficients, owner_lists.T, density[0], velocity[0])
    return out[None]


def solution(mesh):
    in_specs = (
        P("comp", "dom", None, None, None),
        P("comp", None, "dom", None, None, None),
        P(),
        P(),
    )
    out_specs = P("comp", "dom", None, None, None)
    return jax.shard_map(local, mesh=mesh, in_specs=in_specs, out_specs=out_specs, check_vma=False)
```
